128 devices in a mesh: ctx: 32 (over x, z, core), head: 4 (over y).
Axes of the slice: x: 4, y: 4, z: 4, core: 2. Of those that a mesh axis runs over, the one named last changes fastest.
Arguments:
- hidden_in: bfloat16 [16384, 7168], P('ctx', 'head'), may hold values from -6 to 6
- gate_weight: bfloat16 [7168, 192], P('head'), may hold values from -0.09375 to 0.09375
- encoded_queries: bfloat16 [16384, 64, 128], P('ctx', 'head'), may hold values from -12 to 12
- encoded_keys: bfloat16 [16384, 4, 128], P('ctx', 'head'), may hold values from -12 to 12
- value_tensor: bfloat16 [16384, 4, 128], P('ctx', 'head'), may hold values from -6 to 6
- comp_key_weight: float32 [64, 128], replicated, may hold values from -0.75 to 0.75
- comp_value_weight: float32 [64, 128], replicated, may hold values from -0.75 to 0.75
- selection: int32 [256, 4, 16], P('ctx', 'head'), may hold values from 0 to 255, as said below
Outputs:
- attended: bfloat16 [16384, 64, 128], P('ctx', 'head')
The draws below stay inside these ranges and needn't reach their ends.
Inputs may be any that keep to these rules, and one draw needn't show every extreme that they name: `selection`: entries of one list are distinct and the first is the query block's own block. For one index of ctx and one group, the blocks named over all its query blocks that lie in one other index's shard are at most 4, and some index reaches 4 in every draw.
All inputs are finite; a program needn't handle non-finite values.
Results may differ from the reference program's by a relative error of at most 0.011.
Values may be sent and summed in bfloat16 or wider, within the bound.
No kernel may reach another device: no remote copies, remote signals or barrier semaphores. Data moves between devices by JAX's collectives and lax.ppermute only.
A program may use at most 64 MiB of HBM per device.

```python
import jax
import jax.numpy as jnp
from jax import lax

D = 7168
QUERY_HEADS = 64
KEY_VALUE_HEADS = 4
HEAD_SIZE = 128
BLOCK_TOKENS = 64
PICKED_BLOCKS = 16
WINDOW_TOKENS = 512
CONTEXT_TOKENS = 16384
CONTEXT_BLOCKS = 256
BLOCKS_PER_INDEX = 8


def draw_encoded_queries(key, part):
    raw_values = jax.random.normal(jax.random.fold_in(key, 1), (CONTEXT_TOKENS, QUERY_HEADS, HEAD_SIZE), jnp.float32)
    return jnp.clip(raw_values, -12.0, 12.0).astype(jnp.bfloat16)


def draw_encoded_keys(key, part):
    raw_values = jax.random.normal(jax.random.fold_in(key, 11), (CONTEXT_TOKENS, KEY_VALUE_HEADS, HEAD_SIZE), jnp.float32)
    return jnp.clip(raw_values, -12.0, 12.0).astype(jnp.bfloat16)


def draw_selection(key, part):
    shard_parts = CONTEXT_BLOCKS // BLOCKS_PER_INDEX
    capacity = min(BLOCKS_PER_INDEX // 2, PICKED_BLOCKS - 1)
    pooled_scores = jax.random.randint(jax.random.fold_in(key, 21), (shard_parts, shard_parts, KEY_VALUE_HEADS, BLOCKS_PER_INDEX), 0, 1 << 20) * BLOCKS_PER_INDEX + jnp.arange(BLOCKS_PER_INDEX, dtype=jnp.int32)
    order = jnp.argsort(pooled_scores, axis=-1)
    ranks = jnp.argsort(order, axis=-1)
    in_pool = ranks < capacity
    shard_ids = jnp.arange(shard_parts, dtype=jnp.int32)
    popular_blocks_raw = jax.random.randint(jax.random.fold_in(key, 22), (shard_parts, KEY_VALUE_HEADS), 0, 1 << 20)
    hot_owner = popular_blocks_raw % jnp.maximum(shard_ids, 1)[:, None]
    block_ids = jnp.arange(CONTEXT_BLOCKS, dtype=jnp.int32)
    query_dev = block_ids // BLOCKS_PER_INDEX
    owner_dev = block_ids // BLOCKS_PER_INDEX
    local_blk = block_ids % BLOCKS_PER_INDEX
    group_index_list = jnp.arange(KEY_VALUE_HEADS, dtype=jnp.int32)
    pooled = in_pool[query_dev[:, None, None], owner_dev[None, None, :], group_index_list[None, :, None], local_blk[None, None, :]]
    eligible = (owner_dev[None, None, :] == query_dev[:, None, None]) | pooled
    causal = block_ids[None, None, :] <= block_ids[:, None, None]
    hot_match = (owner_dev[None, None, :] == hot_owner[query_dev][:, :, None]) & (owner_dev[None, None, :] != query_dev[:, None, None])
    own_block = block_ids[None, None, :] == block_ids[:, None, None]
    tier = jnp.where(own_block, 8, jnp.where(eligible & hot_match & causal, 4, jnp.where(eligible & causal, 2, jnp.where(eligible, 1, 0))))
    random_noise = jax.random.randint(jax.random.fold_in(key, 23), (CONTEXT_BLOCKS, KEY_VALUE_HEADS, CONTEXT_BLOCKS), 0, 1 << 15)
    scores = tier * (1 << 27) + random_noise * CONTEXT_BLOCKS + block_ids[None, None, :]
    chosen_vals, chosen_blocks = lax.top_k(scores, PICKED_BLOCKS)
    return chosen_blocks.astype(jnp.int32)


def with_spikes(array, rng, source, target, shards_of, factor):
    owner, partner = [(jnp.arange(array.shape[dim]) // (array.shape[dim] // shards_of)).reshape([-1 if axis == dim else 1 for axis in range(array.ndim)]) for dim in (source, target)]
    chosen = jax.random.permutation(rng, shards_of)[partner]
    strong = (owner == chosen) | (owner == (partner + shards_of // 2) % shards_of)
    return jnp.where(strong, factor * array, array)


def levels(stream_key, shape, split, least, high):
    factor_of, own = 1.0, jax.random.fold_in(stream_key, 6)
    for axis_at, blocks in split:
        steps = jnp.exp(jax.random.uniform(jax.random.fold_in(own, axis_at), (blocks,), jnp.float32, least / len(split), high / len(split)))
        factor_of = factor_of * jnp.repeat(steps, shape[axis_at] // blocks).reshape([-1 if axis == axis_at else 1 for axis in range(len(shape))])
    return factor_of


def centred(rng, extent, scale, most, cuts=(), held_as=jnp.bfloat16):
    drawn = jax.random.normal(rng, extent, jnp.float32) * scale
    if len(cuts) > 0:
        drawn = levels(rng, extent, cuts, -0.22, 0.18) * drawn
    return jnp.clip(drawn, min=-most, max=most).astype(held_as)


def heavy_noise(stream_key, dims, scale, limit, shards, heavy, held_as=jnp.bfloat16):
    array = scale * jax.random.normal(stream_key, dims, jnp.float32)
    if shards:
        array = array * levels(stream_key, dims, shards, -0.22, 0.18)
    return jnp.clip(with_spikes(array, jax.random.fold_in(stream_key, 3), *heavy), -limit, limit).astype(held_as)


def setup_inputs(seed: int = 0) -> dict:
    keys = jax.random.split(jax.random.key(seed), 9)
    return {
        "hidden_in": centred(keys[0], (CONTEXT_TOKENS, D), 1.0, 6.0, ((0, 32), (1, 4))),
        "gate_weight": heavy_noise(keys[1], (D, 3 * QUERY_HEADS), D ** -0.5, 0.09375, ((0, 4),), (0, 1, 4, 2.0)),
        "encoded_queries": draw_encoded_queries(jax.random.fold_in(keys[8], 71), 0),
        "encoded_keys": draw_encoded_keys(jax.random.fold_in(keys[8], 71), 0),
        "value_tensor": centred(keys[4], (CONTEXT_TOKENS, KEY_VALUE_HEADS, HEAD_SIZE), 1.0, 6.0, ((0, 32), (1, 4))),
        "comp_key_weight": centred(keys[5], (BLOCK_TOKENS, HEAD_SIZE), BLOCK_TOKENS ** -0.5, 0.75, (), jnp.float32),
        "comp_value_weight": centred(keys[6], (BLOCK_TOKENS, HEAD_SIZE), BLOCK_TOKENS ** -0.5, 0.75, (), jnp.float32),
        "selection": draw_selection(jax.random.fold_in(keys[8], 71), 0),
    }


def attend(query_block_index, key_rows, value_rows, key_mask, with_null):
    scale = query_block_index.shape[-1] ** -0.5
    scores = jnp.einsum("tgjd,gkd->tgjk", query_block_index.astype(jnp.float32), key_rows.astype(jnp.float32), precision=lax.Precision.HIGHEST) * scale
    scores = jnp.where(key_mask[:, :, None, :], scores, -1e30)
    peak = jnp.max(scores, axis=-1, keepdims=True)
    if with_null:
        peak = jnp.maximum(peak, 0.0)
    weights = jnp.exp(scores - peak)
    total_w = jnp.sum(weights, axis=-1, keepdims=True)
    if with_null:
        total_w = total_w + jnp.exp(-peak)
    rounded = (weights / total_w).astype(jnp.bfloat16)
    return jnp.einsum("tgjk,gkd->tgjd", rounded.astype(jnp.float32), value_rows.astype(jnp.float32), precision=lax.Precision.HIGHEST)


def reference(hidden_in, gate_weight, encoded_queries, encoded_keys, value_tensor, comp_key_weight, comp_value_weight, selection):
    block_count_total = CONTEXT_TOKENS // BLOCK_TOKENS
    group_width = QUERY_HEADS // KEY_VALUE_HEADS
    logits = jnp.dot(hidden_in, gate_weight, preferred_element_type=jnp.float32)
    gate_values = jax.nn.sigmoid(logits).reshape(CONTEXT_TOKENS, QUERY_HEADS, 3)
    widened_key_rows = encoded_keys.astype(jnp.float32).reshape(block_count_total, BLOCK_TOKENS, KEY_VALUE_HEADS, HEAD_SIZE)
    widened_value_rows = value_tensor.astype(jnp.float32).reshape(block_count_total, BLOCK_TOKENS, KEY_VALUE_HEADS, HEAD_SIZE)
    comp_keys = jnp.sum(widened_key_rows * comp_key_weight[None, :, None, :], axis=1).transpose(1, 0, 2)
    comp_values = jnp.sum(widened_value_rows * comp_value_weight[None, :, None, :], axis=1).transpose(1, 0, 2)
    comp_ends = (jnp.arange(block_count_total, dtype=jnp.int32) + 1) * BLOCK_TOKENS - 1
    blocked_keys = encoded_keys.reshape(block_count_total, BLOCK_TOKENS, KEY_VALUE_HEADS, HEAD_SIZE).transpose(2, 0, 1, 3)
    blocked_values = value_tensor.reshape(block_count_total, BLOCK_TOKENS, KEY_VALUE_HEADS, HEAD_SIZE).transpose(2, 0, 1, 3)
    padded_key_rows = jnp.concatenate([jnp.zeros((WINDOW_TOKENS, KEY_VALUE_HEADS, HEAD_SIZE), jnp.bfloat16), encoded_keys], axis=0)
    padded_value_rows = jnp.concatenate([jnp.zeros((WINDOW_TOKENS, KEY_VALUE_HEADS, HEAD_SIZE), jnp.bfloat16), value_tensor], axis=0)
    group_index_list = jnp.arange(KEY_VALUE_HEADS, dtype=jnp.int32)[:, None]
    inner_result = jnp.arange(BLOCK_TOKENS, dtype=jnp.int32)

    def per_block(block_num):
        query_start = (block_num * BLOCK_TOKENS).astype(jnp.int32)
        query_block_index = lax.dynamic_slice_in_dim(encoded_queries, query_start, BLOCK_TOKENS, 0).reshape(BLOCK_TOKENS, KEY_VALUE_HEADS, group_width, HEAD_SIZE)
        query_pos = query_start + inner_result
        comp_mask = comp_ends[None, None, :] <= query_pos[:, None, None]
        out_comp = attend(query_block_index, comp_keys, comp_values, comp_mask, True)
        chosen_blocks = selection[block_num]
        selected_keys = blocked_keys[group_index_list, chosen_blocks].reshape(KEY_VALUE_HEADS, PICKED_BLOCKS * BLOCK_TOKENS, HEAD_SIZE)
        selected_values = blocked_values[group_index_list, chosen_blocks].reshape(KEY_VALUE_HEADS, PICKED_BLOCKS * BLOCK_TOKENS, HEAD_SIZE)
        selected_positions = (chosen_blocks[:, :, None] * BLOCK_TOKENS + inner_result[None, None, :]).reshape(KEY_VALUE_HEADS, PICKED_BLOCKS * BLOCK_TOKENS)
        sel_mask = selected_positions[None, :, :] <= query_pos[:, None, None]
        out_sel = attend(query_block_index, selected_keys, selected_values, sel_mask, False)
        win_keys = lax.dynamic_slice_in_dim(padded_key_rows, query_start, WINDOW_TOKENS + BLOCK_TOKENS, 0).transpose(1, 0, 2)
        win_vals = lax.dynamic_slice_in_dim(padded_value_rows, query_start, WINDOW_TOKENS + BLOCK_TOKENS, 0).transpose(1, 0, 2)
        win_pos = query_start - WINDOW_TOKENS + jnp.arange(WINDOW_TOKENS + BLOCK_TOKENS, dtype=jnp.int32)
        win_mask = (win_pos[None, :] <= query_pos[:, None]) & (win_pos[None, :] > query_pos[:, None] - WINDOW_TOKENS) & (win_pos[None, :] >= 0)
        out_win = attend(query_block_index, win_keys, win_vals, win_mask[:, None, :], False)
        gate_block_rows = lax.dynamic_slice_in_dim(gate_values, query_start, BLOCK_TOKENS, 0).reshape(BLOCK_TOKENS, KEY_VALUE_HEADS, group_width, 3)
        merged = gate_block_rows[..., 0:1] * out_comp + gate_block_rows[..., 1:2] * out_sel + gate_block_rows[..., 2:3] * out_win
        return merged.reshape(BLOCK_TOKENS, QUERY_HEADS, HEAD_SIZE).astype(jnp.bfloat16)

    results = lax.map(per_block, jnp.arange(CONTEXT_BLOCKS, dtype=jnp.int32))
    return results.reshape(CONTEXT_TOKENS, QUERY_HEADS, HEAD_SIZE)
```

```python
import functools
import math

import jax
import jax.numpy as jnp
from jax import lax
from jax.experimental import pallas as pl
from jax.experimental.pallas import tpu as pltpu
from jax.sharding import PartitionSpec as P

WINDOW_TOKENS = 512
MASKED = -1e30
LOG2E = 1.4426950408889634
ROW_TILE = 256
NT = (((1,), (1,)), ((), ()))


def shifted(value, axis, steps):
    count = lax.axis_size(axis)
    initial, last = (max(0, -steps), min(count, count - steps))
    return lax.ppermute(value, axis, [(source, source + steps) for source in range(initial, last)])


def token_one_hot(rows, first_row, heads):
    token = (lax.broadcasted_iota(jnp.int32, (rows, 128), 0) + first_row) // heads
    lane = lax.broadcasted_iota(jnp.int32, (rows, 128), 1)
    return jnp.where(token == lane, 1.0, 0.0).astype(jnp.bfloat16)


def softmax_parts(scores, factor):
    peak = jnp.max(scores, axis=-1, keepdims=True)
    return peak, jnp.exp2(scores * factor - peak * factor)


def near_kernel(
    block_len, heads, index_ref, q_ref, kv_ref, summary_hi_ref, summary_lo_ref, comp_ref, win_ref, bias_ref
):
    head_dim = q_ref.shape[-1]
    rows = block_len * heads
    blk = pl.program_id(0)
    factor = LOG2E / math.sqrt(head_dim)
    span = WINDOW_TOKENS + block_len
    own = index_ref[0]
    first = pl.multiple_of(blk * block_len, block_len)
    key = lax.broadcasted_iota(jnp.int32, (span, 128), 0)
    tok = lax.broadcasted_iota(jnp.int32, (span, 128), 1)
    start = own * (kv_ref.shape[0] // 2) + blk * block_len
    seen = (key > tok) & (key <= tok + WINDOW_TOKENS) & (key + start >= WINDOW_TOKENS)
    bias_ref[...] = jnp.where(seen, 0.0, MASKED).astype(jnp.bfloat16)
    keys = jnp.concatenate([kv_ref[pl.ds(first, span), :head_dim], bias_ref[...]], axis=1)
    values = jnp.concatenate(
        [kv_ref[pl.ds(first, span), head_dim:], jnp.ones((span, 128), jnp.bfloat16)], axis=1
    )
    comp_keys = jnp.concatenate([summary_hi_ref[:, :head_dim], summary_lo_ref[:, :head_dim]], axis=1)
    comp_values = jnp.concatenate([summary_hi_ref[:, head_dim:], summary_lo_ref[:, head_dim:]], axis=1)
    count = comp_keys.shape[0]
    block_index = own * (kv_ref.shape[0] // 2 // block_len) + blk
    for at in range(0, rows, ROW_TILE):
        q = q_ref[pl.ds(at, ROW_TILE), :]
        hot = token_one_hot(ROW_TILE, at, heads)
        scores = lax.dot_general(
            jnp.concatenate([q, hot], axis=1), keys, NT, preferred_element_type=jnp.float32
        )
        _, weights = softmax_parts(scores, factor)
        both = jnp.dot(weights.astype(jnp.bfloat16), values, preferred_element_type=jnp.float32)
        win_ref[pl.ds(at, ROW_TILE), :] = both[:, :head_dim] / both[:, head_dim:]
        scores = lax.dot_general(
            jnp.concatenate([q, q], axis=1), comp_keys, NT, preferred_element_type=jnp.float32
        )
        token = (lax.broadcasted_iota(jnp.int32, (ROW_TILE, count), 0) + at) // heads
        limit = block_index + jnp.where(token == block_len - 1, 1, 0)
        lane = lax.broadcasted_iota(jnp.int32, (ROW_TILE, count), 1)
        scores = jnp.where(lane < limit, scores, MASKED)
        peak = jnp.maximum(jnp.max(scores, axis=-1, keepdims=True), 0.0)
        weights = jnp.exp2(scores * factor - peak * factor)
        total = jnp.sum(weights, axis=-1, keepdims=True) + jnp.exp2(-peak * factor)
        both = jnp.dot(weights.astype(jnp.bfloat16), comp_values, preferred_element_type=jnp.float32)
        comp_ref[pl.ds(at, ROW_TILE), :] = (both[:, :head_dim] + both[:, head_dim:]) / total


def far_kernel(
    block_len, heads, picks, pick_ref, index_ref, q_ref, logit_ref, comp_ref, win_ref, all_ref, out_ref,
    kv_ref, bias_ref, sems,
):
    head_dim = q_ref.shape[-1]
    rows = block_len * heads
    blk = pl.program_id(0)
    steps = pl.num_programs(0)
    factor = LOG2E / math.sqrt(head_dim)
    own_block = index_ref[0] * steps + blk
    slot = lax.rem(blk, 2)

    def fetch(step, into, pick):
        source = pl.multiple_of(pick_ref[step * picks + pick] * block_len, block_len)
        return pltpu.make_async_copy(
            all_ref.at[pl.ds(source, block_len), :],
            kv_ref.at[into, pl.ds(pick * block_len, block_len), :],
            sems.at[into, pick],
        )

    @pl.when(blk == 0)
    def _():
        for pick in range(picks):
            fetch(blk, slot, pick).start()

    @pl.when(blk + 1 < steps)
    def _():
        for pick in range(picks):
            fetch(blk + 1, 1 - slot, pick).start()

    key = lax.broadcasted_iota(jnp.int32, (block_len, 128), 0)
    tok = lax.broadcasted_iota(jnp.int32, (block_len, 128), 1)
    for pick in range(picks):
        chosen = pick_ref[blk * picks + pick]
        last = jnp.where(chosen < own_block, block_len, jnp.where(chosen == own_block, 0, -2 * block_len))
        bias_ref[pl.ds(pick * block_len, block_len), :] = jnp.where(
            key <= tok + last, 0.0, MASKED
        ).astype(jnp.bfloat16)
    gate = jax.nn.sigmoid(logit_ref[...])
    columns = gate.shape[1]
    gate_hi = gate.astype(jnp.bfloat16)
    gate_lo = (gate - gate_hi.astype(jnp.float32)).astype(jnp.bfloat16)
    spread = jnp.zeros((128 - block_len, columns), jnp.bfloat16)
    gate_hi = jnp.concatenate([gate_hi, spread], axis=0)
    gate_lo = jnp.concatenate([gate_lo, spread], axis=0)
    for pick in range(picks):
        fetch(blk, slot, pick).wait()
    keys = jnp.concatenate([kv_ref[slot, :, :head_dim], bias_ref[...]], axis=1)
    values = jnp.concatenate(
        [kv_ref[slot, :, head_dim:], jnp.ones((picks * block_len, 128), jnp.bfloat16)], axis=1
    )
    ones = jnp.ones((columns, head_dim), jnp.bfloat16)
    for at in range(0, rows, ROW_TILE):
        q = q_ref[pl.ds(at, ROW_TILE), :]
        hot = token_one_hot(ROW_TILE, at, heads)
        scores = lax.dot_general(
            jnp.concatenate([q, hot], axis=1), keys, NT, preferred_element_type=jnp.float32
        )
        _, weights = softmax_parts(scores, factor)
        both = jnp.dot(weights.astype(jnp.bfloat16), values, preferred_element_type=jnp.float32)
        sel = both[:, :head_dim] / both[:, head_dim:]
        of_token_hi = jnp.dot(hot, gate_hi, preferred_element_type=jnp.float32)
        of_token_lo = jnp.dot(hot, gate_lo, preferred_element_type=jnp.float32)
        head = lax.rem(lax.broadcasted_iota(jnp.int32, (ROW_TILE, columns), 0) + at, heads)
        column = lax.broadcasted_iota(jnp.int32, (ROW_TILE, columns), 1)

        def gate_of(branch):
            mine = column == head * 3 + branch
            return jnp.dot(
                jnp.where(mine, of_token_hi, 0.0).astype(jnp.bfloat16), ones,
                preferred_element_type=jnp.float32,
            ) + jnp.dot(
                jnp.where(mine, of_token_lo, 0.0).astype(jnp.bfloat16), ones,
                preferred_element_type=jnp.float32,
            )

        merged = (
            gate_of(0) * comp_ref[pl.ds(at, ROW_TILE), :]
            + gate_of(1) * sel
            + gate_of(2) * win_ref[pl.ds(at, ROW_TILE), :]
        )
        out_ref[pl.ds(at, ROW_TILE), :] = merged.astype(jnp.bfloat16)


def body(
    hidden_in,
    gate_weight,
    encoded_queries,
    encoded_keys,
    value_tensor,
    comp_key_weight,
    comp_value_weight,
    selection,
):
    rows_here, heads_here, head_dim = encoded_queries.shape
    block_len = comp_key_weight.shape[0]
    picks = selection.shape[-1]
    blocks_here = rows_here // block_len
    shard_parts = lax.axis_size("ctx")
    rows = block_len * heads_here
    index = lax.axis_index("ctx").astype(jnp.int32).reshape(1)

    key_value = jnp.concatenate([encoded_keys, value_tensor], axis=-1).reshape(rows_here, 2 * head_dim)
    gathered = lax.all_gather(key_value, "ctx", axis=0, tiled=True)

    partial_value = jnp.dot(hidden_in, gate_weight, preferred_element_type=jnp.float32)
    logits = lax.psum_scatter(partial_value, "head", scatter_dimension=1, tiled=True)

    widened = key_value.astype(jnp.float32).reshape(blocks_here, block_len, 2 * head_dim)
    compress_w = jnp.concatenate([comp_key_weight, comp_value_weight], axis=-1)
    summary = jnp.sum(widened * compress_w[None, :, :], axis=1)
    summaries = lax.all_gather(summary, "ctx", axis=0, tiled=True)
    summary_hi = summaries.astype(jnp.bfloat16)
    summary_lo = (summaries - summary_hi.astype(jnp.float32)).astype(jnp.bfloat16)
    previous = shifted(key_value, "ctx", 1)
    extended = jnp.concatenate([previous, key_value], axis=0)
    queries = encoded_queries.reshape(rows_here * heads_here, head_dim)
    blocks_total = blocks_here * shard_parts

    tile = pl.BlockSpec((rows, head_dim), lambda b, *_: (b, 0))
    whole = lambda shape: pl.BlockSpec(shape, lambda b, *_: (0, 0))
    branch = jax.ShapeDtypeStruct((rows_here * heads_here, head_dim), jnp.float32)
    comp, win = pl.pallas_call(
        functools.partial(near_kernel, block_len, heads_here),
        out_shape=(branch, branch),
        grid_spec=pltpu.PrefetchScalarGridSpec(
            num_scalar_prefetch=1,
            grid=(blocks_here,),
            in_specs=[
                tile,
                whole((2 * rows_here, 2 * head_dim)),
                whole((blocks_total, 2 * head_dim)),
                whole((blocks_total, 2 * head_dim)),
            ],
            out_specs=(tile, tile),
            scratch_shapes=[pltpu.VMEM((WINDOW_TOKENS + block_len, 128), jnp.bfloat16)],
        ),
        compiler_params=pltpu.CompilerParams(vmem_limit_bytes=40 << 20),
        cost_estimate=pl.CostEstimate(
            flops=4 * rows_here * heads_here * head_dim * 832,
            transcendentals=rows_here * heads_here * 832,
            bytes_accessed=12 << 20,
        ),
        name="near",
    )(index, queries, extended, summary_hi, summary_lo)

    out = pl.pallas_call(
        functools.partial(far_kernel, block_len, heads_here, picks),
        out_shape=jax.ShapeDtypeStruct((rows_here * heads_here, head_dim), jnp.bfloat16),
        grid_spec=pltpu.PrefetchScalarGridSpec(
            num_scalar_prefetch=2,
            grid=(blocks_here,),
            in_specs=[
                tile,
                pl.BlockSpec((block_len, logits.shape[1]), lambda b, *_: (b, 0)),
                tile,
                tile,
                pl.BlockSpec(memory_space=pl.ANY),
            ],
            out_specs=tile,
            scratch_shapes=[
                pltpu.VMEM((2, picks * block_len, 2 * head_dim), jnp.bfloat16),
                pltpu.VMEM((picks * block_len, 128), jnp.bfloat16),
                pltpu.SemaphoreType.DMA((2, picks)),
            ],
        ),
        compiler_params=pltpu.CompilerParams(vmem_limit_bytes=40 << 20),
        cost_estimate=pl.CostEstimate(
            flops=4 * rows_here * heads_here * head_dim * 1024,
            transcendentals=rows_here * heads_here * 1024,
            bytes_accessed=16 << 20,
        ),
        name="far",
    )(selection.reshape(-1), index, queries, logits, comp, win, gathered)
    return out.reshape(rows_here, heads_here, head_dim)


def solution(mesh):
    return jax.shard_map(
        body,
        mesh=mesh,
        in_specs=(
            P("ctx", "head"),
            P("head", None),
            P("ctx", "head", None),
            P("ctx", "head", None),
            P("ctx", "head", None),
            P(),
            P(),
            P("ctx", "head", None),
        ),
        out_specs=P("ctx", "head", None),
        check_vma=False,
    )
```

```python
import functools
import math

import jax
import jax.numpy as jnp
from jax import lax
from jax.experimental import pallas as pl
from jax.experimental.pallas import tpu as pltpu
from jax.sharding import PartitionSpec as P

WINDOW_TOKENS = 512
MASKED = -1e30
LOG2E = 1.4426950408889634
ROW_TILE = 256
SIDE = 4
CORES = 2
NT = (((1,), (1,)), ((), ()))
F32 = jnp.float32
BF16 = jnp.bfloat16


def place(x, z, core):
    return ((x % SIDE) * SIDE + z % SIDE) * CORES + core


def pairs(target):
    spots = [(x, z, c) for x in range(SIDE) for z in range(SIDE) for c in range(CORES)]
    return [(place(*spot), place(*target(*spot))) for spot in spots]


def first_axis(steps):
    return pairs(lambda x, z, c: (x, z + steps, c) if c == 0 else (x + steps, z, c))


def second_axis(steps):
    return pairs(lambda x, z, c: (x + steps, z, c) if c == 0 else (x, z + steps, c))


def other_core():
    return pairs(lambda x, z, c: (x, z, 1 - c))


def in_hbm(value):
    return pltpu.with_memory_space_constraint(value, pltpu.HBM)


def token_one_hot(rows, first_row, heads, first_lane):
    token = (lax.broadcasted_iota(jnp.int32, (rows, 128), 0) + first_row) // heads + first_lane
    lane = lax.broadcasted_iota(jnp.int32, (rows, 128), 1)
    return jnp.where(token == lane, 1.0, 0.0).astype(BF16)


def split(value):
    high = value.astype(BF16)
    return high, (value - high.astype(F32)).astype(BF16)


def near_kernel(
    block_len, heads, index_ref, q_ref, previous_ref, own_ref, logit_ref, win_ref, gate_ref, kv_ref, bias_ref
):
    head_dim = q_ref.shape[-1]
    rows = block_len * heads
    rows_here = own_ref.shape[0]
    blk = pl.program_id(0)
    factor = LOG2E / math.sqrt(head_dim)
    span = WINDOW_TOKENS + block_len

    @pl.when(blk == 0)
    def _():
        kv_ref[pl.ds(0, rows_here), :] = previous_ref[...]
        kv_ref[pl.ds(rows_here, rows_here), :] = own_ref[...]

    first = pl.multiple_of(blk * block_len, block_len)
    key = lax.broadcasted_iota(jnp.int32, (span, 128), 0)
    tok = lax.broadcasted_iota(jnp.int32, (span, 128), 1)
    start = index_ref[0] * rows_here + blk * block_len
    seen = (key > tok) & (key <= tok + WINDOW_TOKENS) & (key + start >= WINDOW_TOKENS)
    bias_ref[...] = jnp.where(seen, 0.0, MASKED).astype(BF16)
    keys = jnp.concatenate([kv_ref[pl.ds(first, span), :head_dim], bias_ref[...]], axis=1)
    values = jnp.concatenate(
        [kv_ref[pl.ds(first, span), head_dim:], jnp.ones((span, 128), BF16)], axis=1
    )
    columns = logit_ref.shape[0]
    gates = jnp.concatenate(split(jax.nn.sigmoid(logit_ref[...])), axis=1)
    tokens_there = logit_ref.shape[1]
    for at in range(0, rows, ROW_TILE):
        q = q_ref[pl.ds(at, ROW_TILE), :]
        hot = token_one_hot(ROW_TILE, at, heads, 0)
        scores = lax.dot_general(
            jnp.concatenate([q, hot], axis=1), keys, NT, preferred_element_type=F32
        )
        peak = jnp.max(scores, axis=-1, keepdims=True)
        weights = jnp.exp2(scores * factor - peak * factor).astype(BF16)
        both = jnp.dot(weights, values, preferred_element_type=F32)
        moved = token_one_hot(ROW_TILE, at, heads, lax.rem(blk, tokens_there // block_len) * block_len)
        of_token = lax.dot_general(
            jnp.concatenate([moved, moved], axis=1), gates, NT, preferred_element_type=F32
        )
        head = lax.rem(lax.broadcasted_iota(jnp.int32, (ROW_TILE, columns), 0) + at, heads)
        column = lax.broadcasted_iota(jnp.int32, (ROW_TILE, columns), 1) - head * 3
        comp_gate, sel_gate, win_gate = [
            jnp.sum(jnp.where(column == branch, of_token, 0.0), axis=-1, keepdims=True)
            for branch in range(3)
        ]
        win_ref[pl.ds(at, ROW_TILE), :] = win_gate * (both[:, :head_dim] / both[:, head_dim:])
        lane = lax.broadcasted_iota(jnp.int32, (ROW_TILE, 128), 1)
        gate_ref[pl.ds(at, ROW_TILE), :] = jnp.where(lane < 64, comp_gate, sel_gate)


def far_kernel(
    block_len, heads, picks, places, pick_ref, row_ref, index_ref, q_ref, gate_ref, win_ref, id_ref, weight_ref,
    *refs,
):
    piece_refs = refs[: len(places)]
    out_ref, all_ref, comp_ref, keys_ref, values_ref, sems = refs[len(places) :]
    head_dim = q_ref.shape[-1]
    rows = block_len * heads
    blk = pl.program_id(0)
    steps = pl.num_programs(0)
    factor = LOG2E / math.sqrt(head_dim)
    own_block = index_ref[0] * steps + blk
    count = all_ref.shape[0] // block_len

    @pl.when(blk == 0)
    def _():
        copies = [
            pltpu.make_async_copy(piece, all_ref.at[pl.ds(at, piece.shape[0]), :], sems.at[n])
            for n, (piece, at) in enumerate(zip(piece_refs, places))
        ]
        for copy in copies:
            copy.start()
        values_ref[:, head_dim:] = jnp.ones((picks * block_len, 128), BF16)
        for copy in copies:
            copy.wait()

        def compress(group, carry):
            parts = []
            for n in range(8):
                base = pl.multiple_of((group * 8 + n) * block_len, block_len)
                block = all_ref[pl.ds(base, block_len), :].astype(F32)
                parts.append(jnp.sum(block * weight_ref[...], axis=0, keepdims=True))
            high, low = split(jnp.concatenate(parts, axis=0))
            at = pl.multiple_of(group * 8, 8)
            comp_ref[0, pl.ds(at, 8), :] = high.astype(F32)
            comp_ref[1, pl.ds(at, 8), :] = low.astype(F32)
            return carry

        lax.fori_loop(0, count // 8, compress, 0)

    key = lax.broadcasted_iota(jnp.int32, (block_len, 128), 0)
    tok = lax.broadcasted_iota(jnp.int32, (block_len, 128), 1)
    for pick in range(picks):
        chosen = pick_ref[blk * picks + pick]
        source = pl.multiple_of(row_ref[blk * picks + pick], block_len)
        into = pl.ds(pick * block_len, block_len)
        last = jnp.where(chosen < own_block, block_len, jnp.where(chosen == own_block, 0, -2 * block_len))
        keys_ref[into, :head_dim] = all_ref[pl.ds(source, block_len), :head_dim]
        values_ref[into, :head_dim] = all_ref[pl.ds(source, block_len), head_dim:]
        keys_ref[into, head_dim:] = jnp.where(key <= tok + last, 0.0, MASKED).astype(BF16)
    comp = comp_ref[...].astype(BF16)
    comp_keys = jnp.concatenate([comp[0, :, :head_dim], comp[1, :, :head_dim]], axis=1)
    comp_values = jnp.concatenate([comp[0, :, head_dim:], comp[1, :, head_dim:]], axis=1)
    for at in range(0, rows, ROW_TILE):
        q = q_ref[pl.ds(at, ROW_TILE), :]
        hot = token_one_hot(ROW_TILE, at, heads, 0)
        scores = lax.dot_general(
            jnp.concatenate([q, hot], axis=1), keys_ref[...], NT, preferred_element_type=F32
        )
        peak = jnp.max(scores, axis=-1, keepdims=True)
        weights = jnp.exp2(scores * factor - peak * factor).astype(BF16)
        both = jnp.dot(weights, values_ref[...], preferred_element_type=F32)
        sel = both[:, :head_dim] / both[:, head_dim:]
        scores = lax.dot_general(
            jnp.concatenate([q, q], axis=1), comp_keys, NT, preferred_element_type=F32
        )
        token = (lax.broadcasted_iota(jnp.int32, (ROW_TILE, 1), 0) + at) // heads
        limit = own_block + jnp.where(token == block_len - 1, 1, 0)
        scores = jnp.where(id_ref[...] < limit, scores, MASKED)
        peak = jnp.maximum(jnp.max(scores, axis=-1, keepdims=True), 0.0)
        weights = jnp.exp2(scores * factor - peak * factor)
        total = jnp.sum(weights, axis=-1, keepdims=True) + jnp.exp2(-peak * factor)
        both = jnp.dot(weights.astype(BF16), comp_values, preferred_element_type=F32)
        gate = gate_ref[pl.ds(at, ROW_TILE), :]
        merged = (
            (gate[:, 0:1] / total) * (both[:, :head_dim] + both[:, head_dim:])
            + gate[:, 64:65] * sel
            + win_ref[pl.ds(at, ROW_TILE), :]
        )
        out_ref[pl.ds(at, ROW_TILE), :] = merged.astype(BF16)


def partial_logits(hidden_in, gate_weight):
    return lax.dot_general(
        gate_weight, hidden_in, (((0,), (1,)), ((), ())), preferred_element_type=F32
    )


def gate_logits(partial_value):
    parts = lax.axis_size("head")
    mine = lax.axis_index("head")
    columns = partial_value.shape[0] // parts

    def chunk(which):
        return lax.dynamic_slice_in_dim(partial_value, lax.rem(which, parts) * columns, columns, 0)

    total = chunk(mine)
    for steps in range(1, parts):
        total = total + lax.ppermute(
            chunk(mine + steps), "head", [(n, (n + steps) % parts) for n in range(parts)]
        )
    return total


def send(value, perm):
    return lax.ppermute(value, "ctx", perm)


def gather_line(key_value, beside):
    ahead = send(key_value, perm=first_axis(-1))
    behind = send(key_value, perm=first_axis(1))
    across = send(key_value, perm=first_axis(2))
    ahead, behind, across, beside = lax.optimization_barrier((ahead, behind, across, beside))
    return jnp.concatenate([key_value, ahead, across, behind], axis=0), beside


def gather_pieces(line, meanwhile):
    half = line.shape[0] // 2
    next_line = send(line, perm=second_axis(-1))
    last_line = send(line, perm=second_axis(1))
    done = meanwhile()
    low, high, done = lax.optimization_barrier((next_line[:half], last_line[half:], done))
    far_low = send(low, perm=second_axis(-1))
    far_high = send(high, perm=second_axis(1))
    rows = line.shape[0]
    mine = [(line, 0), (next_line, rows), (far_low, 2 * rows), (far_high, 2 * rows + half), (last_line, 3 * rows)]
    return mine + [(send(piece, perm=other_core()), at + SIDE * rows) for piece, at in mine], done


def row_of_block(block, index, blocks_here, block_len):
    shard = block // blocks_here
    core = shard % CORES
    across_x = (shard // (SIDE * CORES) - index // (SIDE * CORES)) % SIDE
    across_z = (shard // CORES - index // CORES) % SIDE
    along = jnp.where(core == 0, across_z, across_x)
    line = jnp.where(core == 0, across_x, across_z)
    piece = jnp.where(core == index % CORES, 0, SIDE) + line
    return ((piece * SIDE + along) * blocks_here + block % blocks_here) * block_len


def body(
    hidden_in,
    gate_weight,
    encoded_queries,
    encoded_keys,
    value_tensor,
    comp_key_weight,
    comp_value_weight,
    selection,
):
    rows_here, heads_here, head_dim = encoded_queries.shape
    block_len = comp_key_weight.shape[0]
    picks = selection.shape[-1]
    blocks_here = rows_here // block_len
    shard_parts = lax.axis_size("ctx")
    rows = block_len * heads_here
    all_rows = rows_here * heads_here
    place_here = lax.axis_index("ctx").astype(jnp.int32)
    index = place_here.reshape(1)

    key_value = jnp.concatenate([encoded_keys, value_tensor], axis=-1).reshape(rows_here, 2 * head_dim)
    line, partial_value = gather_line(key_value, partial_logits(hidden_in, gate_weight))
    compress_w = jnp.concatenate([comp_key_weight, comp_value_weight], axis=-1)
    queries = in_hbm(encoded_queries.reshape(all_rows, head_dim))
    total_blocks = blocks_here * shard_parts
    chosen = selection.reshape(-1)
    source_rows = row_of_block(chosen, place_here, blocks_here, block_len)
    block_ids = jnp.arange(total_blocks, dtype=jnp.int32)
    placed = row_of_block(block_ids, place_here, blocks_here, block_len) // block_len
    slots = jnp.arange(total_blocks, dtype=jnp.int32)
    ids_by_slot = jnp.sum(
        jnp.where(placed[None, :] == slots[:, None], block_ids[None, :], 0), axis=1, dtype=jnp.int32
    ).reshape(1, total_blocks)

    tile = pl.BlockSpec((rows, head_dim), lambda b, *_: (b, 0))
    whole = lambda shape: pl.BlockSpec(shape, lambda b, *_: (0, 0))
    wide = pltpu.HBM((all_rows, head_dim), F32)
    def near():
        previous = lax.ppermute(key_value, "ctx", [(n, n + 1) for n in range(shard_parts - 1)])
        logits = gate_logits(partial_value)
        return pl.pallas_call(
            functools.partial(near_kernel, block_len, heads_here),
            out_shape=(wide, wide),
            grid_spec=pltpu.PrefetchScalarGridSpec(
                num_scalar_prefetch=1,
                grid=(blocks_here,),
                in_specs=[
                    tile,
                    whole((rows_here, 2 * head_dim)),
                    whole((rows_here, 2 * head_dim)),
                    pl.BlockSpec((logits.shape[0], 128), lambda b, *_: (0, b * block_len // 128)),
                ],
                out_specs=(tile, tile),
                scratch_shapes=[
                    pltpu.VMEM((2 * rows_here, 2 * head_dim), BF16),
                    pltpu.VMEM((WINDOW_TOKENS + block_len, 128), BF16),
                ],
            ),
            compiler_params=pltpu.CompilerParams(vmem_limit_bytes=56 << 20),
            cost_estimate=pl.CostEstimate(
                flops=4 * all_rows * head_dim * 1024, transcendentals=all_rows * 576, bytes_accessed=12 << 20
            ),
            name="near",
        )(index, queries, previous, key_value, logits)

    pieces, (win, gate) = gather_pieces(line, near)
    out = pl.pallas_call(
        functools.partial(far_kernel, block_len, heads_here, picks, [at for _, at in pieces]),
        out_shape=jax.ShapeDtypeStruct((all_rows, head_dim), BF16),
        grid_spec=pltpu.PrefetchScalarGridSpec(
            num_scalar_prefetch=3,
            grid=(blocks_here,),
            in_specs=[tile, tile, tile, whole((1, total_blocks)), whole((block_len, 2 * head_dim))]
            + [pl.BlockSpec(memory_space=pl.ANY)] * len(pieces),
            out_specs=tile,
            scratch_shapes=[
                pltpu.VMEM((rows_here * shard_parts, 2 * head_dim), BF16),
                pltpu.VMEM((2, total_blocks, 2 * head_dim), F32),
                pltpu.VMEM((picks * block_len, 2 * head_dim), BF16),
                pltpu.VMEM((picks * block_len, 2 * head_dim), BF16),
                pltpu.SemaphoreType.DMA((len(pieces),)),
            ],
        ),
        compiler_params=pltpu.CompilerParams(vmem_limit_bytes=56 << 20),
        cost_estimate=pl.CostEstimate(
            flops=8 * all_rows * head_dim * 1280, transcendentals=all_rows * 1280, bytes_accessed=20 << 20
        ),
        name="far",
    )(
        chosen, source_rows, index, queries, gate, win, ids_by_slot, compress_w,
        *[in_hbm(piece) for piece, _ in pieces],
    )
    return out.reshape(rows_here, heads_here, head_dim)


def solution(mesh):
    return jax.shard_map(
        body,
        mesh=mesh,
        in_specs=(
            P("ctx", "head"),
            P("head", None),
            P("ctx", "head", None),
            P("ctx", "head", None),
            P("ctx", "head", None),
            P(),
            P(),
            P("ctx", "head", None),
        ),
        out_specs=P("ctx", "head", None),
        check_vma=False,
    )
```

```python
import functools
import math

import jax
import jax.numpy as jnp
from jax import lax
from jax.experimental import pallas as pl
from jax.experimental.pallas import tpu as pltpu
from jax.sharding import PartitionSpec as P

WINDOW_TOKENS = 512
MASKED = -1e30
LOG2E = 1.4426950408889634
ROW_TILE = 256
GROUP = 16
NEAR_TOKENS = 128
SIDE = 4
CORES = 2
NT = (((1,), (1,)), ((), ()))
F32 = jnp.float32
BF16 = jnp.bfloat16


def place(x, z, core):
    return ((x % SIDE) * SIDE + z % SIDE) * CORES + core


def pairs(target):
    spots = [(x, z, c) for x in range(SIDE) for z in range(SIDE) for c in range(CORES)]
    return [(place(*spot), place(*target(*spot))) for spot in spots]


def first_axis(steps):
    return pairs(lambda x, z, c: (x, z + steps, c) if c == 0 else (x + steps, z, c))


def second_axis(steps):
    return pairs(lambda x, z, c: (x + steps, z, c) if c == 0 else (x, z + steps, c))


def other_core():
    return pairs(lambda x, z, c: (x, z, 1 - c))


def in_hbm(value):
    return pltpu.with_memory_space_constraint(value, pltpu.HBM)


def token_one_hot(rows, first_row, heads):
    token = (lax.broadcasted_iota(jnp.int32, (rows, 128), 0) + first_row) // heads
    lane = lax.broadcasted_iota(jnp.int32, (rows, 128), 1)
    return jnp.where(token == lane, 1.0, 0.0).astype(BF16)


def split(value):
    high = value.astype(BF16)
    return high, (value - high.astype(F32)).astype(BF16)


def near_kernel(heads, first_step, index_ref, q_ref, previous_ref, own_ref, *refs):
    win_ref, kv_ref, bias_ref = refs[-3:]
    head_dim = q_ref.shape[-1]
    tokens = NEAR_TOKENS
    rows = tokens * heads
    rows_here = own_ref.shape[0]
    step = pl.program_id(0) + first_step
    factor = LOG2E / math.sqrt(head_dim)
    span = WINDOW_TOKENS + tokens
    lead = WINDOW_TOKENS

    @pl.when(pl.program_id(0) == 0)
    def _():
        kv_ref[pl.ds(lead - rows_here, rows_here), :] = previous_ref[...]
        kv_ref[pl.ds(lead, rows_here), :] = own_ref[...]

    first = pl.multiple_of(step * tokens, tokens)
    key = lax.broadcasted_iota(jnp.int32, (span, 128), 0) - lead
    tok = lax.broadcasted_iota(jnp.int32, (span, 128), 1)
    start = index_ref[0] * rows_here + step * tokens
    seen = (key > tok - WINDOW_TOKENS) & (key <= tok) & (key + start >= 0)
    bias_ref[...] = jnp.where(seen, 0.0, MASKED).astype(BF16)
    keys = jnp.concatenate([kv_ref[pl.ds(first, span), :head_dim], bias_ref[...]], axis=1)
    values = jnp.concatenate(
        [kv_ref[pl.ds(first, span), head_dim:], jnp.ones((span, 128), BF16)], axis=1
    )

    def score(at):
        q = jnp.concatenate([q_ref[pl.ds(at, ROW_TILE), :], token_one_hot(ROW_TILE, at, heads)], axis=1)
        return lax.dot_general(q, keys, NT, preferred_element_type=F32)

    ahead = score(0)
    for at in range(0, rows, ROW_TILE):
        scores = ahead
        if at + ROW_TILE < rows:
            ahead = score(at + ROW_TILE)
        peak = jnp.max(scores, axis=-1, keepdims=True)
        weights = jnp.exp2(scores * factor - peak * factor).astype(BF16)
        both = jnp.dot(weights, values, preferred_element_type=F32)
        win_ref[pl.ds(at, ROW_TILE), :] = both[:, :head_dim] / both[:, head_dim:]


def far_kernel(
    block_len, heads, picks, places, pick_ref, row_ref, index_ref, q_ref, logit_ref, win_ref, id_ref, weight_ref,
    *refs,
):
    piece_refs = refs[: len(places)]
    out_ref, all_ref, comp_ref, keys_ref, values_ref, sems = refs[len(places) :]
    head_dim = q_ref.shape[-1]
    rows = block_len * heads
    blk = pl.program_id(0)
    steps = pl.num_programs(0)
    factor = LOG2E / math.sqrt(head_dim)
    own_block = index_ref[0] * steps + blk

    @pl.when(blk == 0)
    def _():
        copies = [
            pltpu.make_async_copy(piece, all_ref.at[pl.ds(at, piece.shape[0]), :], sems.at[n])
            for n, (piece, at) in enumerate(zip(piece_refs, places))
        ]
        for copy in copies:
            copy.start()
        values_ref[:, head_dim:] = jnp.ones((picks * block_len, 128), BF16)

        def compress(group, carry):
            parts = []
            for n in range(GROUP):
                base = pl.multiple_of((group * GROUP + n) * block_len, block_len)
                block = all_ref[pl.ds(base, block_len), :].astype(F32)
                parts.append(jnp.sum(block * weight_ref[...], axis=0, keepdims=True))
            high, low = split(jnp.concatenate(parts, axis=0))
            at = pl.multiple_of(group * GROUP, GROUP)
            comp_ref[0, pl.ds(at, GROUP), :] = high
            comp_ref[1, pl.ds(at, GROUP), :] = low
            return carry

        each = GROUP * block_len
        for copy, piece, at in zip(copies, piece_refs, places):
            copy.wait()
            lax.fori_loop(at // each, (at + piece.shape[0]) // each, compress, 0)

    key = lax.broadcasted_iota(jnp.int32, (block_len, 128), 0)
    tok = lax.broadcasted_iota(jnp.int32, (block_len, 128), 1)
    for pick in range(picks):
        chosen = pick_ref[blk * picks + pick]
        source = pl.multiple_of(row_ref[blk * picks + pick], block_len)
        into = pl.ds(pick * block_len, block_len)
        last = jnp.where(chosen < own_block, block_len, jnp.where(chosen == own_block, 0, -2 * block_len))
        keys_ref[into, :head_dim] = all_ref[pl.ds(source, block_len), :head_dim]
        values_ref[into, :head_dim] = all_ref[pl.ds(source, block_len), head_dim:]
        keys_ref[into, head_dim:] = jnp.where(key <= tok + last, 0.0, MASKED).astype(BF16)
    comp_keys = jnp.concatenate([comp_ref[0, :, :head_dim], comp_ref[1, :, :head_dim]], axis=1)
    comp_values = jnp.concatenate([comp_ref[0, :, head_dim:], comp_ref[1, :, head_dim:]], axis=1)
    gates = jax.nn.sigmoid(logit_ref[0])

    def spread(branch, at):
        return jnp.concatenate(
            [
                jnp.broadcast_to(gates[branch, :, t : t + 1], (heads, 128))
                for t in range(at // heads, (at + ROW_TILE) // heads)
            ],
            axis=0,
        )

    def score(at):
        q = q_ref[pl.ds(at, ROW_TILE), :]
        hot = token_one_hot(ROW_TILE, at, heads)
        sel = lax.dot_general(
            jnp.concatenate([q, hot], axis=1), keys_ref[...], NT, preferred_element_type=F32
        )
        comp = lax.dot_general(
            jnp.concatenate([q, q], axis=1), comp_keys, NT, preferred_element_type=F32
        )
        return sel, comp

    ahead = score(0)
    for at in range(0, rows, ROW_TILE):
        scores, comp_scores = ahead
        if at + ROW_TILE < rows:
            ahead = score(at + ROW_TILE)
        peak = jnp.max(scores, axis=-1, keepdims=True)
        weights = jnp.exp2(scores * factor - peak * factor).astype(BF16)
        both = jnp.dot(weights, values_ref[...], preferred_element_type=F32)
        sel = both[:, :head_dim] / both[:, head_dim:]
        token = (lax.broadcasted_iota(jnp.int32, (ROW_TILE, 1), 0) + at) // heads
        limit = own_block + jnp.where(token == block_len - 1, 1, 0)
        scores = jnp.where(id_ref[...] < limit, comp_scores, MASKED)
        peak = jnp.maximum(jnp.max(scores, axis=-1, keepdims=True), 0.0)
        weights = jnp.exp2(scores * factor - peak * factor)
        total = jnp.sum(weights, axis=-1, keepdims=True) + jnp.exp2(-peak * factor)
        both = jnp.dot(weights.astype(BF16), comp_values, preferred_element_type=F32)
        merged = (
            spread(0, at) * ((both[:, :head_dim] + both[:, head_dim:]) / total)
            + spread(1, at) * sel
            + spread(2, at) * win_ref[pl.ds(at, ROW_TILE), :]
        )
        out_ref[pl.ds(at, ROW_TILE), :] = merged.astype(BF16)


def partial_logits(hidden_in, gate_weight):
    return lax.dot_general(
        gate_weight, hidden_in, (((0,), (1,)), ((), ())), preferred_element_type=F32
    )


def gate_logits(partial_value):
    parts = lax.axis_size("head")
    mine = lax.axis_index("head")
    columns = partial_value.shape[0] // parts

    def chunk(which):
        return lax.dynamic_slice_in_dim(partial_value, lax.rem(which, parts) * columns, columns, 0)

    total = chunk(mine)
    for steps in range(1, parts):
        total = total + lax.ppermute(
            chunk(mine + steps), "head", [(n, (n + steps) % parts) for n in range(parts)]
        )
    return total


def send(value, perm):
    return lax.ppermute(value, "ctx", perm)


def gather_line(key_value):
    ahead = send(key_value, perm=first_axis(-1))
    behind = send(key_value, perm=first_axis(1))
    across = send(key_value, perm=first_axis(2))
    low = jnp.concatenate([key_value, ahead], axis=0)
    high = jnp.concatenate([across, behind], axis=0)
    return low, high


def gather_pieces(low, high, first_work, second_work):
    next_low = send(low, perm=second_axis(-1))
    last_high = send(high, perm=second_axis(1))
    next_high = send(high, perm=second_axis(-1))
    last_low = send(low, perm=second_axis(1))
    next_low, last_high, done = lax.optimization_barrier((next_low, last_high, first_work()))
    far_low = send(next_low, perm=second_axis(-1))
    far_high = send(last_high, perm=second_axis(1))
    far_low, far_high, done = lax.optimization_barrier((far_low, far_high, second_work(done)))
    mine = [low, high, next_low, next_high, far_low, far_high, last_low, last_high]
    return mine + [send(piece, perm=other_core()) for piece in mine], done


def row_of_block(block, index, blocks_here, block_len):
    shard = block // blocks_here
    core = shard % CORES
    across_x = (shard // (SIDE * CORES) - index // (SIDE * CORES)) % SIDE
    across_z = (shard // CORES - index // CORES) % SIDE
    along = jnp.where(core == 0, across_z, across_x)
    line = jnp.where(core == 0, across_x, across_z)
    piece = jnp.where(core == index % CORES, 0, SIDE) + line
    return ((piece * SIDE + along) * blocks_here + block % blocks_here) * block_len


def run_near(index, queries, previous, own, heads, first_step, steps, before=None):
    all_rows, head_dim = queries.shape
    rows_here = own.shape[0]
    whole = pl.BlockSpec((rows_here, 2 * head_dim), lambda b, *_: (0, 0))
    tile = pl.BlockSpec((NEAR_TOKENS * heads, head_dim), lambda b, *_: (b + first_step, 0))
    earlier = [] if before is None else [before]
    return pl.pallas_call(
        functools.partial(near_kernel, heads, first_step),
        out_shape=pltpu.HBM((all_rows, head_dim), F32),
        grid_spec=pltpu.PrefetchScalarGridSpec(
            num_scalar_prefetch=1,
            grid=(steps,),
            in_specs=[tile, whole, whole] + [pl.BlockSpec(memory_space=pl.ANY)] * len(earlier),
            out_specs=tile,
            scratch_shapes=[
                pltpu.VMEM((rows_here + WINDOW_TOKENS, 2 * head_dim), BF16),
                pltpu.VMEM((WINDOW_TOKENS + NEAR_TOKENS, 128), BF16),
            ],
        ),
        input_output_aliases={4: 0} if earlier else {},
        compiler_params=pltpu.CompilerParams(vmem_limit_bytes=56 << 20),
        cost_estimate=pl.CostEstimate(
            flops=steps * 4 * NEAR_TOKENS * heads * head_dim * 1024,
            transcendentals=steps * NEAR_TOKENS * heads * 640,
            bytes_accessed=steps * NEAR_TOKENS * heads * head_dim * 6,
        ),
        name="near",
    )(index, queries, previous, own, *earlier)


def run_far(chosen, source_rows, index, queries, logits, win, ids_by_slot, compress_w, pieces, places):
    all_rows, head_dim = queries.shape
    blocks_here, branches, heads, block_len = logits.shape
    picks = chosen.shape[0] // blocks_here
    total_blocks = ids_by_slot.shape[1]
    tile = pl.BlockSpec((block_len * heads, head_dim), lambda b, *_: (b, 0))
    whole = lambda shape: pl.BlockSpec(shape, lambda b, *_: (0, 0))
    return pl.pallas_call(
        functools.partial(far_kernel, block_len, heads, picks, places),
        out_shape=jax.ShapeDtypeStruct((all_rows, head_dim), BF16),
        grid_spec=pltpu.PrefetchScalarGridSpec(
            num_scalar_prefetch=3,
            grid=(blocks_here,),
            in_specs=[
                tile,
                pl.BlockSpec((1, branches, heads, block_len), lambda b, *_: (b, 0, 0, 0)),
                tile,
                whole((1, total_blocks)),
                whole((block_len, 2 * head_dim)),
            ]
            + [pl.BlockSpec(memory_space=pl.ANY)] * len(pieces),
            out_specs=tile,
            scratch_shapes=[
                pltpu.VMEM((total_blocks * block_len, 2 * head_dim), BF16),
                pltpu.VMEM((2, total_blocks, 2 * head_dim), BF16),
                pltpu.VMEM((picks * block_len, 2 * head_dim), BF16),
                pltpu.VMEM((picks * block_len, 2 * head_dim), BF16),
                pltpu.SemaphoreType.DMA((len(pieces),)),
            ],
        ),
        compiler_params=pltpu.CompilerParams(vmem_limit_bytes=56 << 20),
        cost_estimate=pl.CostEstimate(
            flops=8 * all_rows * head_dim * 1280, transcendentals=all_rows * 1280, bytes_accessed=20 << 20
        ),
        name="far",
    )(chosen, source_rows, index, queries, logits, win, ids_by_slot, compress_w, *[in_hbm(p) for p in pieces])


def body(
    hidden_in,
    gate_weight,
    encoded_queries,
    encoded_keys,
    value_tensor,
    comp_key_weight,
    comp_value_weight,
    selection,
):
    rows_here, heads_here, head_dim = encoded_queries.shape
    block_len = comp_key_weight.shape[0]
    blocks_here = rows_here // block_len
    shard_parts = lax.axis_size("ctx")
    all_rows = rows_here * heads_here
    place_here = lax.axis_index("ctx").astype(jnp.int32)
    index = place_here.reshape(1)

    key_value = jnp.concatenate([encoded_keys, value_tensor], axis=-1).reshape(rows_here, 2 * head_dim)
    low, high = gather_line(key_value)
    previous = send(key_value, perm=[(n, n + 1) for n in range(shard_parts - 1)])
    previous, hidden_in = lax.optimization_barrier((previous, hidden_in))
    logits = gate_logits(partial_logits(hidden_in, gate_weight))
    previous, logits = lax.optimization_barrier((previous, logits))
    compress_w = jnp.concatenate([comp_key_weight, comp_value_weight], axis=-1)
    queries = in_hbm(encoded_queries.reshape(all_rows, head_dim))
    total_blocks = blocks_here * shard_parts
    chosen = selection.reshape(-1)
    source_rows = row_of_block(chosen, place_here, blocks_here, block_len)
    block_ids = jnp.arange(total_blocks, dtype=jnp.int32)
    placed = row_of_block(block_ids, place_here, blocks_here, block_len) // block_len
    slots = jnp.arange(total_blocks, dtype=jnp.int32)
    ids_by_slot = jnp.sum(
        jnp.where(placed[None, :] == slots[:, None], block_ids[None, :], 0), axis=1, dtype=jnp.int32
    ).reshape(1, total_blocks)

    near_steps = rows_here // NEAR_TOKENS // 2
    near = functools.partial(run_near, index, queries, previous, key_value, heads_here)
    pieces, win = gather_pieces(
        low, high, lambda: near(0, near_steps), lambda done: near(near_steps, near_steps, done)
    )
    logits = logits.reshape(heads_here, 3, blocks_here, block_len).transpose(2, 1, 0, 3)

    out = run_far(
        chosen, source_rows, index, queries, logits, win, ids_by_slot, compress_w,
        pieces, [n * low.shape[0] for n in range(len(pieces))],
    )
    return out.reshape(rows_here, heads_here, head_dim)


def solution(mesh):
    return jax.shard_map(
        body,
        mesh=mesh,
        in_specs=(
            P("ctx", "head"),
            P("head", None),
            P("ctx", "head", None),
            P("ctx", "head", None),
            P("ctx", "head", None),
            P(),
            P(),
            P("ctx", "head", None),
        ),
        out_specs=P("ctx", "head", None),
        check_vma=False,
    )
```

```python
import functools
import math

import jax
import jax.numpy as jnp
from jax import lax
from jax.experimental import pallas as pl
from jax.experimental.pallas import tpu as pltpu
from jax.sharding import PartitionSpec as P

WINDOW_TOKENS = 512
MASKED = -1e30
LOG2E = 1.4426950408889634
ROW_TILE = 256
GROUP = 16
NEAR_TOKENS = 128
SAFE_RANGE = 2.0**60
SIDE = 4
CORES = 2
NT = (((1,), (1,)), ((), ()))
F32 = jnp.float32
BF16 = jnp.bfloat16


def place(x, z, core):
    return ((x % SIDE) * SIDE + z % SIDE) * CORES + core


def pairs(target):
    spots = [(x, z, c) for x in range(SIDE) for z in range(SIDE) for c in range(CORES)]
    return [(place(*spot), place(*target(*spot))) for spot in spots]


def first_axis(steps):
    return pairs(lambda x, z, c: (x, z + steps, c) if c == 0 else (x + steps, z, c))


def second_axis(steps):
    return pairs(lambda x, z, c: (x + steps, z, c) if c == 0 else (x, z + steps, c))


def other_core():
    return pairs(lambda x, z, c: (x, z, 1 - c))


def in_hbm(value):
    return pltpu.with_memory_space_constraint(value, pltpu.HBM)


def token_one_hot(rows, first_row, heads):
    token = (lax.broadcasted_iota(jnp.int32, (rows, 128), 0) + first_row) // heads
    lane = lax.broadcasted_iota(jnp.int32, (rows, 128), 1)
    return jnp.where(token == lane, 1.0, 0.0).astype(BF16)


def spread_of(total, inverse):
    return jnp.max(jnp.maximum(total, inverse), axis=0, keepdims=True)


def split(value):
    high = value.astype(BF16)
    return high, (value - high.astype(F32)).astype(BF16)


def window_step(heads, rows_here, step, index_ref, q_ref, kv_ref, bias_ref, win_ref):
    head_dim = q_ref.shape[-1]
    rows = NEAR_TOKENS * heads
    factor = LOG2E / math.sqrt(head_dim)
    span = WINDOW_TOKENS + NEAR_TOKENS
    first = pl.multiple_of(step * NEAR_TOKENS, NEAR_TOKENS)
    key = lax.broadcasted_iota(jnp.int32, (span, 128), 0) - WINDOW_TOKENS
    tok = lax.broadcasted_iota(jnp.int32, (span, 128), 1)
    start = index_ref[0] * rows_here + step * NEAR_TOKENS
    seen = (key > tok - WINDOW_TOKENS) & (key <= tok) & (key + start >= 0)
    bias_ref[...] = jnp.where(seen, 0.0, MASKED).astype(BF16)
    keys = jnp.concatenate([kv_ref[pl.ds(first, span), :head_dim], bias_ref[...]], axis=1)
    values = jnp.concatenate(
        [kv_ref[pl.ds(first, span), head_dim:], jnp.ones((span, 128), BF16)], axis=1
    )

    def score(at):
        q = jnp.concatenate([q_ref[pl.ds(at, ROW_TILE), :], token_one_hot(ROW_TILE, at, heads)], axis=1)
        return lax.dot_general(q, keys, NT, preferred_element_type=F32)

    def finish(at, weights):
        both = jnp.dot(weights.astype(BF16), values, preferred_element_type=F32)
        inverse = 1.0 / both[:, head_dim:]
        win_ref[pl.ds(at, ROW_TILE), :] = both[:, :head_dim] * inverse
        return spread_of(both[:, head_dim:], inverse)

    tiles = range(0, rows, ROW_TILE)
    ahead = score(0)
    range_seen = jnp.zeros((1, 128), F32)
    for at in tiles:
        scores = ahead
        if at + ROW_TILE < rows:
            ahead = score(at + ROW_TILE)
        range_seen = jnp.maximum(range_seen, finish(at, jnp.exp2(scores * factor)))

    @pl.when(jnp.logical_not(jnp.max(range_seen) < SAFE_RANGE))
    def _():
        for at in tiles:
            scores = score(at)
            peak = jnp.max(scores, axis=-1, keepdims=True)
            finish(at, jnp.exp2((scores - peak) * factor))


def near_kernel(heads, index_ref, q_ref, previous_ref, own_ref, win_ref, kv_ref, bias_ref):
    rows_here = own_ref.shape[0]

    @pl.when(pl.program_id(0) == 0)
    def _():
        kv_ref[pl.ds(0, rows_here), :] = previous_ref[...]
        kv_ref[pl.ds(rows_here, rows_here), :] = own_ref[...]

    window_step(heads, rows_here, pl.program_id(0), index_ref, q_ref, kv_ref, bias_ref, win_ref)


def far_kernel(
    block_len, heads, picks, places, pick_ref, row_ref, index_ref, q_ref, logit_ref, win_ref, id_ref, weight_ref,
    *refs,
):
    piece_refs = refs[: len(places)]
    out_ref, all_ref, comp_ref, keys_ref, values_ref, sems = refs[len(places) :]
    head_dim = q_ref.shape[-1]
    rows = block_len * heads
    blk = pl.program_id(0)
    steps = pl.num_programs(0)
    factor = LOG2E / math.sqrt(head_dim)
    own_block = index_ref[0] * steps + blk

    @pl.when(blk == 0)
    def _():
        copies = [
            pltpu.make_async_copy(piece, all_ref.at[pl.ds(at, piece.shape[0]), :], sems.at[n])
            for n, (piece, at) in enumerate(zip(piece_refs, places))
        ]
        for copy in copies:
            copy.start()
        values_ref[:, head_dim:] = jnp.ones((picks * block_len, 128), BF16)

        def compress(group, carry):
            parts = []
            for n in range(GROUP):
                base = pl.multiple_of((group * GROUP + n) * block_len, block_len)
                block = all_ref[pl.ds(base, block_len), :].astype(F32)
                parts.append(jnp.sum(block * weight_ref[...], axis=0, keepdims=True))
            high, low = split(jnp.concatenate(parts, axis=0))
            at = pl.multiple_of(group * GROUP, GROUP)
            comp_ref[0, pl.ds(at, GROUP), :] = high
            comp_ref[1, pl.ds(at, GROUP), :] = low
            return carry

        each = GROUP * block_len
        ready = 0
        for copy, piece, at in zip(copies, piece_refs, places):
            copy.wait()
            there = (at + piece.shape[0]) // each
            lax.fori_loop(ready, there, compress, 0)
            ready = there

    key = lax.broadcasted_iota(jnp.int32, (block_len, 128), 0)
    tok = lax.broadcasted_iota(jnp.int32, (block_len, 128), 1)
    for pick in range(picks):
        chosen = pick_ref[blk * picks + pick]
        source = pl.multiple_of(row_ref[blk * picks + pick], block_len)
        into = pl.ds(pick * block_len, block_len)
        last = jnp.where(chosen < own_block, block_len, jnp.where(chosen == own_block, 0, -2 * block_len))
        keys_ref[into, :head_dim] = all_ref[pl.ds(source, block_len), :head_dim]
        values_ref[into, :head_dim] = all_ref[pl.ds(source, block_len), head_dim:]
        keys_ref[into, head_dim:] = jnp.where(key <= tok + last, 0.0, MASKED).astype(BF16)
    comp_keys = jnp.concatenate([comp_ref[0, :, :head_dim], comp_ref[1, :, :head_dim]], axis=1)
    comp_values = jnp.concatenate([comp_ref[0, :, head_dim:], comp_ref[1, :, head_dim:]], axis=1)
    gates = jax.nn.sigmoid(logit_ref[0])

    def spread(branch, at):
        return jnp.concatenate(
            [
                jnp.broadcast_to(gates[branch, :, t : t + 1], (heads, 128))
                for t in range(at // heads, (at + ROW_TILE) // heads)
            ],
            axis=0,
        )

    def score(at):
        q = q_ref[pl.ds(at, ROW_TILE), :]
        hot = token_one_hot(ROW_TILE, at, heads)
        sel = lax.dot_general(
            jnp.concatenate([q, hot], axis=1), keys_ref[...], NT, preferred_element_type=F32
        )
        comp = lax.dot_general(
            jnp.concatenate([q, q], axis=1), comp_keys, NT, preferred_element_type=F32
        )
        token = (lax.broadcasted_iota(jnp.int32, (ROW_TILE, 1), 0) + at) // heads
        limit = own_block + jnp.where(token == block_len - 1, 1, 0)
        return sel, jnp.where(id_ref[...] < limit, comp, MASKED)

    def finish(at, sel_weights, comp_weights, null_weight):
        both = jnp.dot(sel_weights.astype(BF16), values_ref[...], preferred_element_type=F32)
        inverse = 1.0 / both[:, head_dim:]
        sel = both[:, :head_dim] * inverse
        seen = spread_of(both[:, head_dim:], inverse)
        total = jnp.sum(comp_weights, axis=-1, keepdims=True) + null_weight
        both = jnp.dot(comp_weights.astype(BF16), comp_values, preferred_element_type=F32)
        merged = (
            spread(0, at) * ((both[:, :head_dim] + both[:, head_dim:]) / total)
            + spread(1, at) * sel
            + spread(2, at) * win_ref[pl.ds(at, ROW_TILE), :]
        )
        out_ref[pl.ds(at, ROW_TILE), :] = merged.astype(BF16)
        return jnp.maximum(seen, jnp.max(total, axis=0, keepdims=True))

    tiles = range(0, rows, ROW_TILE)
    ahead = score(0)
    range_seen = jnp.zeros((1, 128), F32)
    for at in tiles:
        sel_scores, comp_scores = ahead
        if at + ROW_TILE < rows:
            ahead = score(at + ROW_TILE)
        seen = finish(at, jnp.exp2(sel_scores * factor), jnp.exp2(comp_scores * factor), 1.0)
        range_seen = jnp.maximum(range_seen, seen)

    @pl.when(jnp.logical_not(jnp.max(range_seen) < SAFE_RANGE))
    def _():
        for at in tiles:
            sel_scores, comp_scores = score(at)
            sel_peak = jnp.max(sel_scores, axis=-1, keepdims=True)
            comp_peak = jnp.maximum(jnp.max(comp_scores, axis=-1, keepdims=True), 0.0)
            finish(
                at,
                jnp.exp2((sel_scores - sel_peak) * factor),
                jnp.exp2((comp_scores - comp_peak) * factor),
                jnp.exp2(-comp_peak * factor),
            )


def partial_logits(hidden_in, gate_weight):
    return lax.dot_general(
        gate_weight, hidden_in, (((0,), (1,)), ((), ())), preferred_element_type=F32
    )


def gate_logits(partial_value):
    parts = lax.axis_size("head")
    mine = lax.axis_index("head")
    total = partial_value
    apart = parts // 2
    while apart:
        kept = lax.rem(mine // apart, 2)
        half = total.shape[0] // 2
        sent = lax.dynamic_slice_in_dim(total, (1 - kept) * half, half, 0)
        got = lax.ppermute(sent, "head", [(n, n ^ apart) for n in range(parts)])
        total = lax.dynamic_slice_in_dim(total, kept * half, half, 0) + got
        apart //= 2
    return total


def send(value, perm):
    return lax.ppermute(value, "ctx", perm)


def gather_line(key_value):
    ahead = send(key_value, perm=first_axis(-1))
    behind = send(key_value, perm=first_axis(1))
    across = send(key_value, perm=first_axis(2))
    return [key_value, ahead, across, behind]


def gather_pieces(line, meanwhile, beside):
    line = jnp.concatenate(line, axis=0)
    next_line = send(line, perm=second_axis(-1))
    last_line = send(line, perm=second_axis(1))
    done = meanwhile()
    next_line, last_line, again, done = lax.optimization_barrier((next_line, last_line, line, done))
    across_line = send(again, perm=second_axis(2))
    across_line, small = lax.optimization_barrier((across_line, beside(done)))
    mine = [line, next_line, across_line, last_line]
    pieces = mine + [send(piece, perm=other_core()) for piece in mine]
    return pieces, [n * line.shape[0] for n in range(len(pieces))], small, done


def row_of_block(block, index, blocks_here, block_len):
    shard = block // blocks_here
    core = shard % CORES
    across_x = (shard // (SIDE * CORES) - index // (SIDE * CORES)) % SIDE
    across_z = (shard // CORES - index // CORES) % SIDE
    along = jnp.where(core == 0, across_z, across_x)
    line = jnp.where(core == 0, across_x, across_z)
    piece = jnp.where(core == index % CORES, 0, SIDE) + line
    return ((piece * SIDE + along) * blocks_here + block % blocks_here) * block_len


def run_near(index, queries, previous, own, heads):
    all_rows, head_dim = queries.shape
    rows_here = own.shape[0]
    whole = pl.BlockSpec((rows_here, 2 * head_dim), lambda b, *_: (0, 0))
    tile = pl.BlockSpec((NEAR_TOKENS * heads, head_dim), lambda b, *_: (b, 0))
    steps = rows_here // NEAR_TOKENS
    return pl.pallas_call(
        functools.partial(near_kernel, heads),
        out_shape=pltpu.HBM((all_rows, head_dim), F32),
        grid_spec=pltpu.PrefetchScalarGridSpec(
            num_scalar_prefetch=1,
            grid=(steps,),
            in_specs=[tile, whole, whole],
            out_specs=tile,
            scratch_shapes=[
                pltpu.VMEM((rows_here + WINDOW_TOKENS, 2 * head_dim), BF16),
                pltpu.VMEM((WINDOW_TOKENS + NEAR_TOKENS, 128), BF16),
            ],
        ),
        compiler_params=pltpu.CompilerParams(vmem_limit_bytes=24 << 20),
        cost_estimate=pl.CostEstimate(
            flops=steps * 8 * NEAR_TOKENS * heads * head_dim * 1024,
            transcendentals=0,
            bytes_accessed=steps * NEAR_TOKENS * heads * head_dim * 6,
        ),
        name="near",
    )(index, queries, previous, own)


def run_far(chosen, source_rows, index, queries, logits, win, ids_by_slot, compress_w, pieces, places):
    all_rows, head_dim = queries.shape
    blocks_here, branches, heads, block_len = logits.shape
    picks = chosen.shape[0] // blocks_here
    total_blocks = ids_by_slot.shape[1]
    tile = pl.BlockSpec((block_len * heads, head_dim), lambda b, *_: (b, 0))
    whole = lambda shape: pl.BlockSpec(shape, lambda b, *_: (0, 0))
    return pl.pallas_call(
        functools.partial(far_kernel, block_len, heads, picks, places),
        out_shape=jax.ShapeDtypeStruct((all_rows, head_dim), BF16),
        grid_spec=pltpu.PrefetchScalarGridSpec(
            num_scalar_prefetch=3,
            grid=(blocks_here,),
            in_specs=[
                tile,
                pl.BlockSpec((1, branches, heads, block_len), lambda b, *_: (b, 0, 0, 0)),
                tile,
                whole((1, total_blocks)),
                whole((block_len, 2 * head_dim)),
            ]
            + [pl.BlockSpec(memory_space=pl.ANY)] * len(pieces),
            out_specs=tile,
            scratch_shapes=[
                pltpu.VMEM((total_blocks * block_len, 2 * head_dim), BF16),
                pltpu.VMEM((2, total_blocks, 2 * head_dim), BF16),
                pltpu.VMEM((picks * block_len, 2 * head_dim), BF16),
                pltpu.VMEM((picks * block_len, 2 * head_dim), BF16),
                pltpu.SemaphoreType.DMA((len(pieces),)),
            ],
        ),
        compiler_params=pltpu.CompilerParams(vmem_limit_bytes=56 << 20),
        cost_estimate=pl.CostEstimate(
            flops=8 * all_rows * head_dim * 1280, transcendentals=all_rows * 1280, bytes_accessed=20 << 20
        ),
        name="far",
    )(
        chosen, source_rows, index, queries, logits, win, ids_by_slot, compress_w,
        *[in_hbm(piece) for piece in pieces],
    )


def body(
    hidden_in,
    gate_weight,
    encoded_queries,
    encoded_keys,
    value_tensor,
    comp_key_weight,
    comp_value_weight,
    selection,
):
    rows_here, heads_here, head_dim = encoded_queries.shape
    block_len = comp_key_weight.shape[0]
    blocks_here = rows_here // block_len
    shard_parts = lax.axis_size("ctx")
    all_rows = rows_here * heads_here
    place_here = lax.axis_index("ctx").astype(jnp.int32)
    index = place_here.reshape(1)

    key_value = jnp.concatenate([encoded_keys, value_tensor], axis=-1).reshape(rows_here, 2 * head_dim)
    line = gather_line(key_value)
    previous = send(key_value, perm=[(n, n + 1) for n in range(shard_parts - 1)])
    compress_w = jnp.concatenate([comp_key_weight, comp_value_weight], axis=-1)
    queries = in_hbm(encoded_queries.reshape(all_rows, head_dim))
    total_blocks = blocks_here * shard_parts
    chosen = selection.reshape(-1)
    source_rows = row_of_block(chosen, place_here, blocks_here, block_len)
    block_ids = jnp.arange(total_blocks, dtype=jnp.int32)
    placed = row_of_block(block_ids, place_here, blocks_here, block_len) // block_len
    slots = jnp.arange(total_blocks, dtype=jnp.int32)
    ids_by_slot = jnp.sum(
        jnp.where(placed[None, :] == slots[:, None], block_ids[None, :], 0), axis=1, dtype=jnp.int32
    ).reshape(1, total_blocks)

    near = functools.partial(run_near, index, queries, previous, key_value, heads_here)

    def late_inputs(win):
        after, _ = lax.optimization_barrier((hidden_in, win))
        logits = gate_logits(partial_logits(after, gate_weight))
        logits = logits.reshape(heads_here, 3, blocks_here, block_len).transpose(2, 1, 0, 3)
        return chosen, source_rows, logits, ids_by_slot, compress_w

    pieces, places, (picked, picked_rows, logits, slot_ids, weights), win = gather_pieces(line, near, late_inputs)
    out = run_far(picked, picked_rows, index, queries, logits, win, slot_ids, weights, pieces, places)
    return out.reshape(rows_here, heads_here, head_dim)


def solution(mesh):
    return jax.shard_map(
        body,
        mesh=mesh,
        in_specs=(
            P("ctx", "head"),
            P("head", None),
            P("ctx", "head", None),
            P("ctx", "head", None),
            P("ctx", "head", None),
            P(),
            P(),
            P("ctx", "head", None),
        ),
        out_specs=P("ctx", "head", None),
        check_vma=False,
    )
```

```python
import functools
import math

import jax
import jax.numpy as jnp
from jax import lax
from jax.experimental import pallas as pl
from jax.experimental.pallas import tpu as pltpu
from jax.sharding import PartitionSpec as P

WINDOW_TOKENS = 512
MASKED = -1e30
LOG2E = 1.4426950408889634
ROW_TILE = 256
GROUP = 16
NEAR_TOKENS = 128
SAFE_RANGE = 2.0**60
SIDE = 4
CORES = 2
NT = (((1,), (1,)), ((), ()))
F32 = jnp.float32
BF16 = jnp.bfloat16


def place(x, z, core):
    return ((x % SIDE) * SIDE + z % SIDE) * CORES + core


def pairs(target):
    spots = [(x, z, c) for x in range(SIDE) for z in range(SIDE) for c in range(CORES)]
    return [(place(*spot), place(*target(*spot))) for spot in spots]


def first_axis(steps):
    return pairs(lambda x, z, c: (x, z + steps, c) if c == 0 else (x + steps, z, c))


def second_axis(steps):
    return pairs(lambda x, z, c: (x + steps, z, c) if c == 0 else (x, z + steps, c))


def other_core():
    return pairs(lambda x, z, c: (x, z, 1 - c))


def in_hbm(value):
    return pltpu.with_memory_space_constraint(value, pltpu.HBM)


def token_one_hot(rows, first_row, heads):
    token = (lax.broadcasted_iota(jnp.int32, (rows, 128), 0) + first_row) // heads
    lane = lax.broadcasted_iota(jnp.int32, (rows, 128), 1)
    return jnp.where(token == lane, 1.0, 0.0).astype(BF16)


def spread_of(total, inverse):
    return jnp.max(jnp.maximum(total, inverse), axis=0, keepdims=True)


def split(value):
    high = value.astype(BF16)
    return high, (value - high.astype(F32)).astype(BF16)


def window_step(heads, rows_here, step, index_ref, q_ref, kv_ref, bias_ref, win_ref):
    head_dim = q_ref.shape[-1]
    rows = NEAR_TOKENS * heads
    factor = LOG2E / math.sqrt(head_dim)
    span = WINDOW_TOKENS + NEAR_TOKENS
    first = pl.multiple_of(step * NEAR_TOKENS, NEAR_TOKENS)
    key = lax.broadcasted_iota(jnp.int32, (span, 128), 0) - WINDOW_TOKENS
    tok = lax.broadcasted_iota(jnp.int32, (span, 128), 1)
    start = index_ref[0] * rows_here + step * NEAR_TOKENS
    seen = (key > tok - WINDOW_TOKENS) & (key <= tok) & (key + start >= 0)
    bias_ref[...] = jnp.where(seen, 0.0, MASKED).astype(BF16)
    keys = jnp.concatenate([kv_ref[pl.ds(first, span), :head_dim], bias_ref[...]], axis=1)
    values = jnp.concatenate(
        [kv_ref[pl.ds(first, span), head_dim:], jnp.ones((span, 128), BF16)], axis=1
    )

    def score(at):
        q = jnp.concatenate([q_ref[pl.ds(at, ROW_TILE), :], token_one_hot(ROW_TILE, at, heads)], axis=1)
        return lax.dot_general(q, keys, NT, preferred_element_type=F32)

    def finish(at, weights):
        both = jnp.dot(weights.astype(BF16), values, preferred_element_type=F32)
        inverse = 1.0 / both[:, head_dim:]
        win_ref[pl.ds(at, ROW_TILE), :] = both[:, :head_dim] * inverse
        return spread_of(both[:, head_dim:], inverse)

    tiles = range(0, rows, ROW_TILE)
    ahead = score(0)
    range_seen = jnp.zeros((1, 128), F32)
    for at in tiles:
        scores = ahead
        if at + ROW_TILE < rows:
            ahead = score(at + ROW_TILE)
        range_seen = jnp.maximum(range_seen, finish(at, jnp.exp2(scores * factor)))

    @pl.when(jnp.logical_not(jnp.max(range_seen) < SAFE_RANGE))
    def _():
        for at in tiles:
            scores = score(at)
            peak = jnp.max(scores, axis=-1, keepdims=True)
            finish(at, jnp.exp2((scores - peak) * factor))


def near_kernel(heads, index_ref, q_ref, previous_ref, own_ref, win_ref, kv_ref, bias_ref):
    rows_here = own_ref.shape[0]

    @pl.when(pl.program_id(0) == 0)
    def _():
        kv_ref[pl.ds(0, rows_here), :] = previous_ref[...]
        kv_ref[pl.ds(rows_here, rows_here), :] = own_ref[...]

    window_step(heads, rows_here, pl.program_id(0), index_ref, q_ref, kv_ref, bias_ref, win_ref)


def far_kernel(
    block_len, heads, picks, places, pick_ref, row_ref, index_ref, q_ref, logit_ref, win_ref, id_ref, weight_ref,
    *refs,
):
    piece_refs = refs[: len(places)]
    out_ref, all_ref, comp_ref, keys_ref, values_ref, sems = refs[len(places) :]
    head_dim = q_ref.shape[-1]
    rows = block_len * heads
    blk = pl.program_id(0)
    steps = pl.num_programs(0)
    factor = LOG2E / math.sqrt(head_dim)
    own_block = index_ref[0] * steps + blk

    @pl.when(blk == 0)
    def _():
        copies = [
            pltpu.make_async_copy(piece, all_ref.at[pl.ds(at, piece.shape[0]), :], sems.at[n])
            for n, (piece, at) in enumerate(zip(piece_refs, places))
        ]
        for copy in copies:
            copy.start()
        values_ref[:, head_dim:] = jnp.ones((picks * block_len, 128), BF16)

        def compress(group, carry):
            parts = []
            for n in range(GROUP):
                base = pl.multiple_of((group * GROUP + n) * block_len, block_len)
                block = all_ref[pl.ds(base, block_len), :].astype(F32)
                parts.append(jnp.sum(block * weight_ref[...], axis=0, keepdims=True))
            high, low = split(jnp.concatenate(parts, axis=0))
            at = pl.multiple_of(group * GROUP, GROUP)
            comp_ref[0, pl.ds(at, GROUP), :] = high
            comp_ref[1, pl.ds(at, GROUP), :] = low
            return carry

        each = GROUP * block_len
        ready = 0
        for copy, piece, at in zip(copies, piece_refs, places):
            copy.wait()
            there = (at + piece.shape[0]) // each
            lax.fori_loop(ready, there, compress, 0)
            ready = there

    key = lax.broadcasted_iota(jnp.int32, (block_len, 128), 0)
    tok = lax.broadcasted_iota(jnp.int32, (block_len, 128), 1)
    for pick in range(picks):
        chosen = pick_ref[blk * picks + pick]
        source = pl.multiple_of(row_ref[blk * picks + pick], block_len)
        into = pl.ds(pick * block_len, block_len)
        last = jnp.where(chosen < own_block, block_len, jnp.where(chosen == own_block, 0, -2 * block_len))
        keys_ref[into, :head_dim] = all_ref[pl.ds(source, block_len), :head_dim]
        values_ref[into, :head_dim] = all_ref[pl.ds(source, block_len), head_dim:]
        keys_ref[into, head_dim:] = jnp.where(key <= tok + last, 0.0, MASKED).astype(BF16)
    comp_keys = jnp.concatenate([comp_ref[0, :, :head_dim], comp_ref[1, :, :head_dim]], axis=1)
    comp_values = jnp.concatenate([comp_ref[0, :, head_dim:], comp_ref[1, :, head_dim:]], axis=1)
    gates = jax.nn.sigmoid(logit_ref[0])

    def spread(branch, at):
        return jnp.concatenate(
            [
                jnp.broadcast_to(gates[branch, :, t : t + 1], (heads, 128))
                for t in range(at // heads, (at + ROW_TILE) // heads)
            ],
            axis=0,
        )

    def score(at):
        q = q_ref[pl.ds(at, ROW_TILE), :]
        hot = token_one_hot(ROW_TILE, at, heads)
        sel = lax.dot_general(
            jnp.concatenate([q, hot], axis=1), keys_ref[...], NT, preferred_element_type=F32
        )
        comp = lax.dot_general(
            jnp.concatenate([q, q], axis=1), comp_keys, NT, preferred_element_type=F32
        )
        token = (lax.broadcasted_iota(jnp.int32, (ROW_TILE, 1), 0) + at) // heads
        limit = own_block + jnp.where(token == block_len - 1, 1, 0)
        return sel, jnp.where(id_ref[...] < limit, comp, MASKED)

    def finish(at, sel_weights, comp_weights, null_weight):
        both = jnp.dot(sel_weights.astype(BF16), values_ref[...], preferred_element_type=F32)
        inverse = 1.0 / both[:, head_dim:]
        sel = both[:, :head_dim] * inverse
        seen = spread_of(both[:, head_dim:], inverse)
        total = jnp.sum(comp_weights, axis=-1, keepdims=True) + null_weight
        both = jnp.dot(comp_weights.astype(BF16), comp_values, preferred_element_type=F32)
        merged = (
            spread(0, at) * ((both[:, :head_dim] + both[:, head_dim:]) / total)
            + spread(1, at) * sel
            + spread(2, at) * win_ref[pl.ds(at, ROW_TILE), :]
        )
        out_ref[pl.ds(at, ROW_TILE), :] = merged.astype(BF16)
        return jnp.maximum(seen, jnp.max(total, axis=0, keepdims=True))

    tiles = range(0, rows, ROW_TILE)
    ahead = score(0)
    range_seen = jnp.zeros((1, 128), F32)
    for at in tiles:
        sel_scores, comp_scores = ahead
        if at + ROW_TILE < rows:
            ahead = score(at + ROW_TILE)
        seen = finish(at, jnp.exp2(sel_scores * factor), jnp.exp2(comp_scores * factor), 1.0)
        range_seen = jnp.maximum(range_seen, seen)

    @pl.when(jnp.logical_not(jnp.max(range_seen) < SAFE_RANGE))
    def _():
        for at in tiles:
            sel_scores, comp_scores = score(at)
            sel_peak = jnp.max(sel_scores, axis=-1, keepdims=True)
            comp_peak = jnp.maximum(jnp.max(comp_scores, axis=-1, keepdims=True), 0.0)
            finish(
                at,
                jnp.exp2((sel_scores - sel_peak) * factor),
                jnp.exp2((comp_scores - comp_peak) * factor),
                jnp.exp2(-comp_peak * factor),
            )


def partial_logits(hidden_in, gate_weight):
    return lax.dot_general(
        gate_weight, hidden_in, (((0,), (1,)), ((), ())), preferred_element_type=F32
    )


def gate_logits(partial_value):
    parts = lax.axis_size("head")
    mine = lax.axis_index("head")
    total = partial_value
    apart = parts // 2
    while apart:
        kept = lax.rem(mine // apart, 2)
        half = total.shape[0] // 2
        sent = lax.dynamic_slice_in_dim(total, (1 - kept) * half, half, 0)
        got = lax.ppermute(sent, "head", [(n, n ^ apart) for n in range(parts)])
        total = lax.dynamic_slice_in_dim(total, kept * half, half, 0) + got
        apart //= 2
    return total


def send(value, perm):
    return lax.ppermute(value, "ctx", perm)


def gather_line(key_value):
    ahead = send(key_value, perm=first_axis(-1))
    behind = send(key_value, perm=first_axis(1))
    across = send(key_value, perm=first_axis(2))
    return [key_value, ahead, across, behind]


def gather_pieces(line, meanwhile, beside):
    line = jnp.concatenate(line, axis=0)
    next_line = send(line, perm=second_axis(-1))
    last_line = send(line, perm=second_axis(1))
    done = meanwhile()
    next_line, last_line, again, done = lax.optimization_barrier((next_line, last_line, line, done))
    across_line = send(again, perm=second_axis(2))
    across_line, small = lax.optimization_barrier((across_line, beside(done)))
    mine = [line, next_line, across_line, last_line]
    pieces = mine + [send(piece, perm=other_core()) for piece in mine]
    return pieces, [n * line.shape[0] for n in range(len(pieces))], small, done


def row_of_block(block, index, blocks_here, block_len):
    shard = block // blocks_here
    core = shard % CORES
    across_x = (shard // (SIDE * CORES) - index // (SIDE * CORES)) % SIDE
    across_z = (shard // CORES - index // CORES) % SIDE
    along = jnp.where(core == 0, across_z, across_x)
    line = jnp.where(core == 0, across_x, across_z)
    piece = jnp.where(core == index % CORES, 0, SIDE) + line
    return ((piece * SIDE + along) * blocks_here + block % blocks_here) * block_len


def run_near(index, queries, previous, own, heads):
    all_rows, head_dim = queries.shape
    rows_here = own.shape[0]
    whole = pl.BlockSpec((rows_here, 2 * head_dim), lambda b, *_: (0, 0))
    tile = pl.BlockSpec((NEAR_TOKENS * heads, head_dim), lambda b, *_: (b, 0))
    steps = rows_here // NEAR_TOKENS
    return pl.pallas_call(
        functools.partial(near_kernel, heads),
        out_shape=pltpu.HBM((all_rows, head_dim), F32),
        grid_spec=pltpu.PrefetchScalarGridSpec(
            num_scalar_prefetch=1,
            grid=(steps,),
            in_specs=[tile, whole, whole],
            out_specs=tile,
            scratch_shapes=[
                pltpu.VMEM((rows_here + WINDOW_TOKENS, 2 * head_dim), BF16),
                pltpu.VMEM((WINDOW_TOKENS + NEAR_TOKENS, 128), BF16),
            ],
        ),
        compiler_params=pltpu.CompilerParams(vmem_limit_bytes=24 << 20),
        cost_estimate=pl.CostEstimate(
            flops=steps * 8 * NEAR_TOKENS * heads * head_dim * 1024,
            transcendentals=0,
            bytes_accessed=steps * NEAR_TOKENS * heads * head_dim * 6,
        ),
        name="near",
    )(index, queries, previous, own)


def run_far(chosen, source_rows, index, queries, logits, win, ids_by_slot, compress_w, pieces, places):
    all_rows, head_dim = queries.shape
    blocks_here, branches, heads, block_len = logits.shape
    picks = chosen.shape[0] // blocks_here
    total_blocks = ids_by_slot.shape[1]
    tile = pl.BlockSpec((block_len * heads, head_dim), lambda b, *_: (b, 0))
    whole = lambda shape: pl.BlockSpec(shape, lambda b, *_: (0, 0))
    return pl.pallas_call(
        functools.partial(far_kernel, block_len, heads, picks, places),
        out_shape=jax.ShapeDtypeStruct((all_rows, head_dim), BF16),
        grid_spec=pltpu.PrefetchScalarGridSpec(
            num_scalar_prefetch=3,
            grid=(blocks_here,),
            in_specs=[
                tile,
                pl.BlockSpec((1, branches, heads, block_len), lambda b, *_: (b, 0, 0, 0)),
                tile,
                whole((1, total_blocks)),
                whole((block_len, 2 * head_dim)),
            ]
            + [pl.BlockSpec(memory_space=pl.ANY)] * len(pieces),
            out_specs=tile,
            scratch_shapes=[
                pltpu.VMEM((total_blocks * block_len, 2 * head_dim), BF16),
                pltpu.VMEM((2, total_blocks, 2 * head_dim), BF16),
                pltpu.VMEM((picks * block_len, 2 * head_dim), BF16),
                pltpu.VMEM((picks * block_len, 2 * head_dim), BF16),
                pltpu.SemaphoreType.DMA((len(pieces),)),
            ],
        ),
        compiler_params=pltpu.CompilerParams(vmem_limit_bytes=28 << 20),
        cost_estimate=pl.CostEstimate(
            flops=8 * all_rows * head_dim * 1280, transcendentals=all_rows * 1280, bytes_accessed=20 << 20
        ),
        name="far",
    )(
        chosen, source_rows, index, queries, logits, in_hbm(win), ids_by_slot, compress_w,
        *pieces,
    )


def body(
    hidden_in,
    gate_weight,
    encoded_queries,
    encoded_keys,
    value_tensor,
    comp_key_weight,
    comp_value_weight,
    selection,
):
    rows_here, heads_here, head_dim = encoded_queries.shape
    block_len = comp_key_weight.shape[0]
    blocks_here = rows_here // block_len
    shard_parts = lax.axis_size("ctx")
    all_rows = rows_here * heads_here
    place_here = lax.axis_index("ctx").astype(jnp.int32)
    index = place_here.reshape(1)

    key_value = jnp.concatenate([encoded_keys, value_tensor], axis=-1).reshape(rows_here, 2 * head_dim)
    line = gather_line(key_value)
    previous = send(key_value, perm=[(n, n + 1) for n in range(shard_parts - 1)])
    compress_w = jnp.concatenate([comp_key_weight, comp_value_weight], axis=-1)
    queries = in_hbm(encoded_queries.reshape(all_rows, head_dim))
    total_blocks = blocks_here * shard_parts
    chosen = selection.reshape(-1)
    source_rows = row_of_block(chosen, place_here, blocks_here, block_len)
    block_ids = jnp.arange(total_blocks, dtype=jnp.int32)
    placed = row_of_block(block_ids, place_here, blocks_here, block_len) // block_len
    slots = jnp.arange(total_blocks, dtype=jnp.int32)
    ids_by_slot = jnp.sum(
        jnp.where(placed[None, :] == slots[:, None], block_ids[None, :], 0), axis=1, dtype=jnp.int32
    ).reshape(1, total_blocks)

    near = functools.partial(run_near, index, queries, previous, key_value, heads_here)

    def late_inputs(win):
        after, _ = lax.optimization_barrier((hidden_in, win))
        logits = gate_logits(partial_logits(after, gate_weight))
        logits = logits.reshape(heads_here, 3, blocks_here, block_len).transpose(2, 1, 0, 3)
        return chosen, source_rows, logits, ids_by_slot, compress_w

    pieces, places, (picked, picked_rows, logits, slot_ids, weights), win = gather_pieces(line, near, late_inputs)
    out = run_far(picked, picked_rows, index, queries, logits, win, slot_ids, weights, pieces, places)
    return out.reshape(rows_here, heads_here, head_dim)


def solution(mesh):
    return jax.shard_map(
        body,
        mesh=mesh,
        in_specs=(
            P("ctx", "head"),
            P("head", None),
            P("ctx", "head", None),
            P("ctx", "head", None),
            P("ctx", "head", None),
            P(),
            P(),
            P("ctx", "head", None),
        ),
        out_specs=P("ctx", "head", None),
        check_vma=False,
    )
```

```python
import functools
import math

import jax
import jax.numpy as jnp
from jax import lax
from jax.experimental import pallas as pl
from jax.experimental.pallas import tpu as pltpu
from jax.sharding import PartitionSpec as P

WINDOW_TOKENS = 512
MASKED = -1e30
LOG2E = 1.4426950408889634
ROW_TILE = 512
GROUP = 16
NEAR_TOKENS = 128
SAFE_RANGE = 2.0**60
SIDE = 4
CORES = 2
NT = (((1,), (1,)), ((), ()))
F32 = jnp.float32
BF16 = jnp.bfloat16


def place(x, z, core):
    return ((x % SIDE) * SIDE + z % SIDE) * CORES + core


def pairs(target):
    spots = [(x, z, c) for x in range(SIDE) for z in range(SIDE) for c in range(CORES)]
    return [(place(*spot), place(*target(*spot))) for spot in spots]


def first_axis(steps):
    return pairs(lambda x, z, c: (x, z + steps, c) if c == 0 else (x + steps, z, c))


def second_axis(steps):
    return pairs(lambda x, z, c: (x + steps, z, c) if c == 0 else (x, z + steps, c))


def other_core():
    return pairs(lambda x, z, c: (x, z, 1 - c))


def in_hbm(value):
    return pltpu.with_memory_space_constraint(value, pltpu.HBM)


def token_one_hot(rows, first_row, heads):
    token = (lax.broadcasted_iota(jnp.int32, (rows, 128), 0) + first_row) // heads
    lane = lax.broadcasted_iota(jnp.int32, (rows, 128), 1)
    return jnp.where(token == lane, 1.0, 0.0).astype(BF16)


def spread_of(total, inverse):
    return jnp.max(jnp.maximum(total, inverse), axis=0, keepdims=True)


def split(value):
    high = value.astype(BF16)
    return high, (value - high.astype(F32)).astype(BF16)


def window_step(heads, rows_here, step, index_ref, q_ref, kv_ref, bias_ref, win_ref):
    head_dim = q_ref.shape[-1]
    rows = NEAR_TOKENS * heads
    factor = LOG2E / math.sqrt(head_dim)
    span = WINDOW_TOKENS + NEAR_TOKENS
    first = pl.multiple_of(step * NEAR_TOKENS, NEAR_TOKENS)
    key = lax.broadcasted_iota(jnp.int32, (span, 128), 0) - WINDOW_TOKENS
    tok = lax.broadcasted_iota(jnp.int32, (span, 128), 1)
    start = index_ref[0] * rows_here + step * NEAR_TOKENS
    seen = (key > tok - WINDOW_TOKENS) & (key <= tok) & (key + start >= 0)
    bias_ref[...] = jnp.where(seen, 0.0, MASKED).astype(BF16)
    keys = jnp.concatenate([kv_ref[pl.ds(first, span), :head_dim], bias_ref[...]], axis=1)
    values = jnp.concatenate(
        [kv_ref[pl.ds(first, span), head_dim:], jnp.ones((span, 128), BF16)], axis=1
    )

    def score(at):
        q = jnp.concatenate([q_ref[pl.ds(at, ROW_TILE), :], token_one_hot(ROW_TILE, at, heads)], axis=1)
        return lax.dot_general(q, keys, NT, preferred_element_type=F32)

    def finish(at, weights):
        both = jnp.dot(weights.astype(BF16), values, preferred_element_type=F32)
        inverse = 1.0 / both[:, head_dim:]
        win_ref[pl.ds(at, ROW_TILE), :] = both[:, :head_dim] * inverse
        return spread_of(both[:, head_dim:], inverse)

    tiles = range(0, rows, ROW_TILE)
    ahead = score(0)
    range_seen = jnp.zeros((1, 128), F32)
    for at in tiles:
        scores = ahead
        if at + ROW_TILE < rows:
            ahead = score(at + ROW_TILE)
        range_seen = jnp.maximum(range_seen, finish(at, jnp.exp2(scores * factor)))

    @pl.when(jnp.logical_not(jnp.max(range_seen) < SAFE_RANGE))
    def _():
        for at in tiles:
            scores = score(at)
            peak = jnp.max(scores, axis=-1, keepdims=True)
            finish(at, jnp.exp2((scores - peak) * factor))


def near_kernel(heads, index_ref, q_ref, previous_ref, own_ref, win_ref, kv_ref, bias_ref):
    rows_here = own_ref.shape[0]

    @pl.when(pl.program_id(0) == 0)
    def _():
        kv_ref[pl.ds(0, rows_here), :] = previous_ref[...]
        kv_ref[pl.ds(rows_here, rows_here), :] = own_ref[...]

    window_step(heads, rows_here, pl.program_id(0), index_ref, q_ref, kv_ref, bias_ref, win_ref)


def far_kernel(
    block_len, heads, picks, places, pick_ref, row_ref, index_ref, q_ref, logit_ref, win_ref, id_ref, weight_ref,
    *refs,
):
    piece_refs = refs[: len(places)]
    out_ref, all_ref, comp_ref, keys_ref, values_ref, sems = refs[len(places) :]
    head_dim = q_ref.shape[-1]
    rows = block_len * heads
    blk = pl.program_id(0)
    steps = pl.num_programs(0)
    factor = LOG2E / math.sqrt(head_dim)
    own_block = index_ref[0] * steps + blk

    @pl.when(blk == 0)
    def _():
        copies = [
            pltpu.make_async_copy(piece, all_ref.at[pl.ds(at, piece.shape[0]), :], sems.at[n])
            for n, (piece, at) in enumerate(zip(piece_refs, places))
        ]
        for copy in copies:
            copy.start()
        values_ref[:, head_dim:] = jnp.ones((picks * block_len, 128), BF16)

        def compress(group, carry):
            parts = []
            for n in range(GROUP):
                base = pl.multiple_of((group * GROUP + n) * block_len, block_len)
                block = all_ref[pl.ds(base, block_len), :].astype(F32)
                parts.append(jnp.sum(block * weight_ref[...], axis=0, keepdims=True))
            high, low = split(jnp.concatenate(parts, axis=0))
            at = pl.multiple_of(group * GROUP, GROUP)
            comp_ref[0, pl.ds(at, GROUP), :] = high
            comp_ref[1, pl.ds(at, GROUP), :] = low
            return carry

        each = GROUP * block_len
        ready = 0
        for copy, piece, at in zip(copies, piece_refs, places):
            copy.wait()
            there = (at + piece.shape[0]) // each
            lax.fori_loop(ready, there, compress, 0)
            ready = there

    key = lax.broadcasted_iota(jnp.int32, (block_len, 128), 0)
    tok = lax.broadcasted_iota(jnp.int32, (block_len, 128), 1)
    for pick in range(picks):
        chosen = pick_ref[blk * picks + pick]
        source = pl.multiple_of(row_ref[blk * picks + pick], block_len)
        into = pl.ds(pick * block_len, block_len)
        last = jnp.where(chosen < own_block, block_len, jnp.where(chosen == own_block, 0, -2 * block_len))
        keys_ref[into, :head_dim] = all_ref[pl.ds(source, block_len), :head_dim]
        values_ref[into, :head_dim] = all_ref[pl.ds(source, block_len), head_dim:]
        keys_ref[into, head_dim:] = jnp.where(key <= tok + last, 0.0, MASKED).astype(BF16)
    comp_keys = jnp.concatenate([comp_ref[0, :, :head_dim], comp_ref[1, :, :head_dim]], axis=1)
    comp_values = jnp.concatenate([comp_ref[0, :, head_dim:], comp_ref[1, :, head_dim:]], axis=1)
    gates = jax.nn.sigmoid(logit_ref[0])

    def spread(branch, at):
        return jnp.concatenate(
            [
                jnp.broadcast_to(gates[branch, :, t : t + 1], (heads, 128))
                for t in range(at // heads, (at + ROW_TILE) // heads)
            ],
            axis=0,
        )

    def score(at):
        q = q_ref[pl.ds(at, ROW_TILE), :]
        hot = token_one_hot(ROW_TILE, at, heads)
        sel = lax.dot_general(
            jnp.concatenate([q, hot], axis=1), keys_ref[...], NT, preferred_element_type=F32
        )
        comp = lax.dot_general(
            jnp.concatenate([q, q], axis=1), comp_keys, NT, preferred_element_type=F32
        )
        token = (lax.broadcasted_iota(jnp.int32, (ROW_TILE, 1), 0) + at) // heads
        limit = own_block + jnp.where(token == block_len - 1, 1, 0)
        return sel, jnp.where(id_ref[...] < limit, comp, MASKED)

    def finish(at, sel_weights, comp_weights, null_weight):
        both = jnp.dot(sel_weights.astype(BF16), values_ref[...], preferred_element_type=F32)
        inverse = 1.0 / both[:, head_dim:]
        sel = both[:, :head_dim] * inverse
        seen = spread_of(both[:, head_dim:], inverse)
        total = jnp.sum(comp_weights, axis=-1, keepdims=True) + null_weight
        both = jnp.dot(comp_weights.astype(BF16), comp_values, preferred_element_type=F32)
        merged = (
            spread(0, at) * ((both[:, :head_dim] + both[:, head_dim:]) / total)
            + spread(1, at) * sel
            + spread(2, at) * win_ref[pl.ds(at, ROW_TILE), :]
        )
        out_ref[pl.ds(at, ROW_TILE), :] = merged.astype(BF16)
        return jnp.maximum(seen, jnp.max(total, axis=0, keepdims=True))

    tiles = range(0, rows, ROW_TILE)
    ahead = score(0)
    range_seen = jnp.zeros((1, 128), F32)
    for at in tiles:
        sel_scores, comp_scores = ahead
        if at + ROW_TILE < rows:
            ahead = score(at + ROW_TILE)
        seen = finish(at, jnp.exp2(sel_scores * factor), jnp.exp2(comp_scores * factor), 1.0)
        range_seen = jnp.maximum(range_seen, seen)

    @pl.when(jnp.logical_not(jnp.max(range_seen) < SAFE_RANGE))
    def _():
        for at in tiles:
            sel_scores, comp_scores = score(at)
            sel_peak = jnp.max(sel_scores, axis=-1, keepdims=True)
            comp_peak = jnp.maximum(jnp.max(comp_scores, axis=-1, keepdims=True), 0.0)
            finish(
                at,
                jnp.exp2((sel_scores - sel_peak) * factor),
                jnp.exp2((comp_scores - comp_peak) * factor),
                jnp.exp2(-comp_peak * factor),
            )


def partial_logits(hidden_in, gate_weight):
    return lax.dot_general(
        gate_weight, hidden_in, (((0,), (1,)), ((), ())), preferred_element_type=F32
    )


def gate_logits(partial_value):
    parts = lax.axis_size("head")
    mine = lax.axis_index("head")
    columns = partial_value.shape[0] // parts

    def chunk(which):
        return lax.dynamic_slice_in_dim(partial_value, lax.rem(which, parts) * columns, columns, 0)

    others = [
        lax.ppermute(chunk(mine + steps), "head", [(n, (n + steps) % parts) for n in range(parts)])
        for steps in range(1, parts)
    ]
    others = lax.optimization_barrier(others)
    return chunk(mine) + others[0] + others[1] + others[2]


def send(value, perm):
    return lax.ppermute(value, "ctx", perm)


def gather_line(key_value):
    ahead = send(key_value, perm=first_axis(-1))
    behind = send(key_value, perm=first_axis(1))
    across = send(key_value, perm=first_axis(2))
    return [key_value, ahead, across, behind]


def gather_pieces(line, meanwhile, beside):
    line = jnp.concatenate(line, axis=0)
    next_line = send(line, perm=second_axis(-1))
    last_line = send(line, perm=second_axis(1))
    done = meanwhile()
    next_line, last_line, again, done = lax.optimization_barrier((next_line, last_line, line, done))
    across_line = send(again, perm=second_axis(2))
    across_line, small = lax.optimization_barrier((across_line, beside(done)))
    mine = [line, next_line, across_line, last_line]
    pieces = mine + [send(piece, perm=other_core()) for piece in mine]
    return pieces, [n * line.shape[0] for n in range(len(pieces))], small, done


def row_of_block(block, index, blocks_here, block_len):
    shard = block // blocks_here
    core = shard % CORES
    across_x = (shard // (SIDE * CORES) - index // (SIDE * CORES)) % SIDE
    across_z = (shard // CORES - index // CORES) % SIDE
    along = jnp.where(core == 0, across_z, across_x)
    line = jnp.where(core == 0, across_x, across_z)
    piece = jnp.where(core == index % CORES, 0, SIDE) + line
    return ((piece * SIDE + along) * blocks_here + block % blocks_here) * block_len


def run_near(index, queries, previous, own, heads):
    all_rows, head_dim = queries.shape
    rows_here = own.shape[0]
    whole = pl.BlockSpec((rows_here, 2 * head_dim), lambda b, *_: (0, 0))
    tile = pl.BlockSpec((NEAR_TOKENS * heads, head_dim), lambda b, *_: (b, 0))
    steps = rows_here // NEAR_TOKENS
    return pl.pallas_call(
        functools.partial(near_kernel, heads),
        out_shape=pltpu.HBM((all_rows, head_dim), F32),
        grid_spec=pltpu.PrefetchScalarGridSpec(
            num_scalar_prefetch=1,
            grid=(steps,),
            in_specs=[tile, whole, whole],
            out_specs=tile,
            scratch_shapes=[
                pltpu.VMEM((rows_here + WINDOW_TOKENS, 2 * head_dim), BF16),
                pltpu.VMEM((WINDOW_TOKENS + NEAR_TOKENS, 128), BF16),
            ],
        ),
        compiler_params=pltpu.CompilerParams(vmem_limit_bytes=24 << 20),
        cost_estimate=pl.CostEstimate(
            flops=steps * 8 * NEAR_TOKENS * heads * head_dim * 1024,
            transcendentals=0,
            bytes_accessed=steps * NEAR_TOKENS * heads * head_dim * 6,
        ),
        name="near",
    )(index, queries, previous, own)


def run_far(chosen, source_rows, index, queries, logits, win, ids_by_slot, compress_w, pieces, places):
    all_rows, head_dim = queries.shape
    blocks_here, branches, heads, block_len = logits.shape
    picks = chosen.shape[0] // blocks_here
    total_blocks = ids_by_slot.shape[1]
    tile = pl.BlockSpec((block_len * heads, head_dim), lambda b, *_: (b, 0))
    whole = lambda shape: pl.BlockSpec(shape, lambda b, *_: (0, 0))
    return pl.pallas_call(
        functools.partial(far_kernel, block_len, heads, picks, places),
        out_shape=jax.ShapeDtypeStruct((all_rows, head_dim), BF16),
        grid_spec=pltpu.PrefetchScalarGridSpec(
            num_scalar_prefetch=3,
            grid=(blocks_here,),
            in_specs=[
                tile,
                pl.BlockSpec((1, branches, heads, block_len), lambda b, *_: (b, 0, 0, 0)),
                tile,
                whole((1, total_blocks)),
                whole((block_len, 2 * head_dim)),
            ]
            + [pl.BlockSpec(memory_space=pl.ANY)] * len(pieces),
            out_specs=tile,
            scratch_shapes=[
                pltpu.VMEM((total_blocks * block_len, 2 * head_dim), BF16),
                pltpu.VMEM((2, total_blocks, 2 * head_dim), BF16),
                pltpu.VMEM((picks * block_len, 2 * head_dim), BF16),
                pltpu.VMEM((picks * block_len, 2 * head_dim), BF16),
                pltpu.SemaphoreType.DMA((len(pieces),)),
            ],
        ),
        compiler_params=pltpu.CompilerParams(vmem_limit_bytes=28 << 20),
        cost_estimate=pl.CostEstimate(
            flops=8 * all_rows * head_dim * 1280, transcendentals=all_rows * 1280, bytes_accessed=20 << 20
        ),
        name="far",
    )(
        chosen, source_rows, index, queries, logits, in_hbm(win), ids_by_slot, compress_w,
        *pieces,
    )


def body(
    hidden_in,
    gate_weight,
    encoded_queries,
    encoded_keys,
    value_tensor,
    comp_key_weight,
    comp_value_weight,
    selection,
):
    rows_here, heads_here, head_dim = encoded_queries.shape
    block_len = comp_key_weight.shape[0]
    blocks_here = rows_here // block_len
    shard_parts = lax.axis_size("ctx")
    all_rows = rows_here * heads_here
    place_here = lax.axis_index("ctx").astype(jnp.int32)
    index = place_here.reshape(1)

    key_value = jnp.concatenate([encoded_keys, value_tensor], axis=-1).reshape(rows_here, 2 * head_dim)
    line = gather_line(key_value)
    previous = send(key_value, perm=[(n, n + 1) for n in range(shard_parts - 1)])
    compress_w = jnp.concatenate([comp_key_weight, comp_value_weight], axis=-1)
    queries = in_hbm(encoded_queries.reshape(all_rows, head_dim))
    total_blocks = blocks_here * shard_parts
    chosen = selection.reshape(-1)
    source_rows = row_of_block(chosen, place_here, blocks_here, block_len)
    block_ids = jnp.arange(total_blocks, dtype=jnp.int32)
    placed = row_of_block(block_ids, place_here, blocks_here, block_len) // block_len
    slots = jnp.arange(total_blocks, dtype=jnp.int32)
    ids_by_slot = jnp.sum(
        jnp.where(placed[None, :] == slots[:, None], block_ids[None, :], 0), axis=1, dtype=jnp.int32
    ).reshape(1, total_blocks)

    near = functools.partial(run_near, index, queries, previous, key_value, heads_here)

    def late_inputs(win):
        after, _ = lax.optimization_barrier((hidden_in, win))
        logits = gate_logits(partial_logits(after, gate_weight))
        logits = logits.reshape(heads_here, 3, blocks_here, block_len).transpose(2, 1, 0, 3)
        return chosen, source_rows, logits, ids_by_slot, compress_w

    pieces, places, (picked, picked_rows, logits, slot_ids, weights), win = gather_pieces(line, near, late_inputs)
    out = run_far(picked, picked_rows, index, queries, logits, win, slot_ids, weights, pieces, places)
    return out.reshape(rows_here, heads_here, head_dim)


def solution(mesh):
    return jax.shard_map(
        body,
        mesh=mesh,
        in_specs=(
            P("ctx", "head"),
            P("head", None),
            P("ctx", "head", None),
            P("ctx", "head", None),
            P("ctx", "head", None),
            P(),
            P(),
            P("ctx", "head", None),
        ),
        out_specs=P("ctx", "head", None),
        check_vma=False,
    )
```

```python
import functools
import math

import jax
import jax.numpy as jnp
from jax import lax
from jax.experimental import pallas as pl
from jax.experimental.pallas import tpu as pltpu
from jax.sharding import PartitionSpec as P

WINDOW_TOKENS = 512
MASKED = -1e30
LOG2E = 1.4426950408889634
ROW_TILE = 512
GROUP = 16
NEAR_TOKENS = 128
SAFE_RANGE = 2.0**60
SIDE = 4
CORES = 2
NT = (((1,), (1,)), ((), ()))
F32 = jnp.float32
BF16 = jnp.bfloat16


def place(x, z, core):
    return ((x % SIDE) * SIDE + z % SIDE) * CORES + core


def pairs(target):
    spots = [(x, z, c) for x in range(SIDE) for z in range(SIDE) for c in range(CORES)]
    return [(place(*spot), place(*target(*spot))) for spot in spots]


def first_axis(steps):
    return pairs(lambda x, z, c: (x, z + steps, c) if c == 0 else (x + steps, z, c))


def second_axis(steps):
    return pairs(lambda x, z, c: (x + steps, z, c) if c == 0 else (x, z + steps, c))


def other_core():
    return pairs(lambda x, z, c: (x, z, 1 - c))


def in_hbm(value):
    return pltpu.with_memory_space_constraint(value, pltpu.HBM)


def token_one_hot(rows, first_row, heads):
    token = (lax.broadcasted_iota(jnp.int32, (rows, 128), 0) + first_row) // heads
    lane = lax.broadcasted_iota(jnp.int32, (rows, 128), 1)
    return jnp.where(token == lane, 1.0, 0.0).astype(BF16)


def spread_of(total, inverse):
    return jnp.max(jnp.maximum(total, inverse), axis=0, keepdims=True)


def split(value):
    high = value.astype(BF16)
    return high, (value - high.astype(F32)).astype(BF16)


def window_step(heads, rows_here, step, index_ref, q_ref, kv_ref, bias_ref, win_ref):
    head_dim = q_ref.shape[-1]
    rows = NEAR_TOKENS * heads
    factor = LOG2E / math.sqrt(head_dim)
    span = WINDOW_TOKENS + NEAR_TOKENS
    first = pl.multiple_of(step * NEAR_TOKENS, NEAR_TOKENS)
    key = lax.broadcasted_iota(jnp.int32, (span, 128), 0) - WINDOW_TOKENS
    tok = lax.broadcasted_iota(jnp.int32, (span, 128), 1)
    start = index_ref[0] * rows_here + step * NEAR_TOKENS
    seen = (key > tok - WINDOW_TOKENS) & (key <= tok) & (key + start >= 0)
    bias_ref[...] = jnp.where(seen, 0.0, MASKED).astype(BF16)
    keys = jnp.concatenate([kv_ref[pl.ds(first, span), :head_dim], bias_ref[...]], axis=1)
    values = jnp.concatenate(
        [kv_ref[pl.ds(first, span), head_dim:], jnp.ones((span, 128), BF16)], axis=1
    )

    def score(at):
        q = jnp.concatenate([q_ref[pl.ds(at, ROW_TILE), :], token_one_hot(ROW_TILE, at, heads)], axis=1)
        return lax.dot_general(q, keys, NT, preferred_element_type=F32)

    def finish(at, weights):
        both = jnp.dot(weights.astype(BF16), values, preferred_element_type=F32)
        inverse = 1.0 / both[:, head_dim:]
        win_ref[pl.ds(at, ROW_TILE), :] = both[:, :head_dim] * inverse
        return spread_of(both[:, head_dim:], inverse)

    tiles = range(0, rows, ROW_TILE)
    ahead = score(0)
    range_seen = jnp.zeros((1, 128), F32)
    for at in tiles:
        scores = ahead
        if at + ROW_TILE < rows:
            ahead = score(at + ROW_TILE)
        range_seen = jnp.maximum(range_seen, finish(at, jnp.exp2(scores * factor)))

    @pl.when(jnp.logical_not(jnp.max(range_seen) < SAFE_RANGE))
    def _():
        for at in tiles:
            scores = score(at)
            peak = jnp.max(scores, axis=-1, keepdims=True)
            finish(at, jnp.exp2((scores - peak) * factor))


def near_kernel(heads, index_ref, q_ref, previous_ref, own_ref, win_ref, kv_ref, bias_ref):
    rows_here = own_ref.shape[0]

    @pl.when(pl.program_id(0) == 0)
    def _():
        kv_ref[pl.ds(0, rows_here), :] = previous_ref[...]
        kv_ref[pl.ds(rows_here, rows_here), :] = own_ref[...]

    window_step(heads, rows_here, pl.program_id(0), index_ref, q_ref, kv_ref, bias_ref, win_ref)


def far_kernel(
    block_len, heads, picks, places, pick_ref, row_ref, index_ref, q_ref, logit_ref, win_ref, id_ref, weight_ref,
    *refs,
):
    piece_refs = refs[: len(places)]
    out_ref, all_ref, comp_ref, keys_ref, values_ref, sems = refs[len(places) :]
    head_dim = q_ref.shape[-1]
    rows = block_len * heads
    blk = pl.program_id(0)
    steps = pl.num_programs(0)
    factor = LOG2E / math.sqrt(head_dim)
    own_block = index_ref[0] * steps + blk

    @pl.when(blk == 0)
    def _():
        copies = [
            pltpu.make_async_copy(piece, all_ref.at[pl.ds(at, piece.shape[0]), :], sems.at[n])
            for n, (piece, at) in enumerate(zip(piece_refs, places))
        ]
        for copy in copies:
            copy.start()
        values_ref[:, head_dim:] = jnp.ones((picks * block_len, 128), BF16)

        def compress(group, carry):
            parts = []
            for n in range(GROUP):
                base = pl.multiple_of((group * GROUP + n) * block_len, block_len)
                block = all_ref[pl.ds(base, block_len), :].astype(F32)
                parts.append(jnp.sum(block * weight_ref[...], axis=0, keepdims=True))
            high, low = split(jnp.concatenate(parts, axis=0))
            at = pl.multiple_of(group * GROUP, GROUP)
            comp_ref[0, pl.ds(at, GROUP), :] = high
            comp_ref[1, pl.ds(at, GROUP), :] = low
            return carry

        each = GROUP * block_len
        ready = 0
        for copy, piece, at in zip(copies, piece_refs, places):
            copy.wait()
            there = (at + piece.shape[0]) // each
            lax.fori_loop(ready, there, compress, 0)
            ready = there

    key = lax.broadcasted_iota(jnp.int32, (block_len, 128), 0)
    tok = lax.broadcasted_iota(jnp.int32, (block_len, 128), 1)
    for pick in range(picks):
        chosen = pick_ref[blk * picks + pick]
        source = pl.multiple_of(row_ref[blk * picks + pick], block_len)
        into = pl.ds(pick * block_len, block_len)
        last = jnp.where(chosen < own_block, block_len, jnp.where(chosen == own_block, 0, -2 * block_len))
        keys_ref[into, :head_dim] = all_ref[pl.ds(source, block_len), :head_dim]
        values_ref[into, :head_dim] = all_ref[pl.ds(source, block_len), head_dim:]
        keys_ref[into, head_dim:] = jnp.where(key <= tok + last, 0.0, MASKED).astype(BF16)
    comp_keys = jnp.concatenate([comp_ref[0, :, :head_dim], comp_ref[1, :, :head_dim]], axis=1)
    comp_values = jnp.concatenate([comp_ref[0, :, head_dim:], comp_ref[1, :, head_dim:]], axis=1)
    gates = jax.nn.sigmoid(logit_ref[0])

    def spread(branch, at):
        return jnp.concatenate(
            [
                jnp.broadcast_to(gates[branch, :, t : t + 1], (heads, 128))
                for t in range(at // heads, (at + ROW_TILE) // heads)
            ],
            axis=0,
        )

    def score(at):
        q = q_ref[pl.ds(at, ROW_TILE), :]
        hot = token_one_hot(ROW_TILE, at, heads)
        sel = lax.dot_general(
            jnp.concatenate([q, hot], axis=1), keys_ref[...], NT, preferred_element_type=F32
        )
        comp = lax.dot_general(
            jnp.concatenate([q, q], axis=1), comp_keys, NT, preferred_element_type=F32
        )
        token = (lax.broadcasted_iota(jnp.int32, (ROW_TILE, 1), 0) + at) // heads
        limit = own_block + jnp.where(token == block_len - 1, 1, 0)
        return sel, jnp.where(id_ref[...] < limit, comp, MASKED)

    def finish(at, sel_weights, comp_weights, null_weight):
        both = jnp.dot(sel_weights.astype(BF16), values_ref[...], preferred_element_type=F32)
        inverse = 1.0 / both[:, head_dim:]
        sel = both[:, :head_dim] * inverse
        seen = spread_of(both[:, head_dim:], inverse)
        total = jnp.sum(comp_weights, axis=-1, keepdims=True) + null_weight
        both = jnp.dot(comp_weights.astype(BF16), comp_values, preferred_element_type=F32)
        merged = (
            spread(0, at) * ((both[:, :head_dim] + both[:, head_dim:]) / total)
            + spread(1, at) * sel
            + spread(2, at) * win_ref[pl.ds(at, ROW_TILE), :]
        )
        out_ref[pl.ds(at, ROW_TILE), :] = merged.astype(BF16)
        return jnp.maximum(seen, jnp.max(total, axis=0, keepdims=True))

    tiles = range(0, rows, ROW_TILE)
    ahead = score(0)
    range_seen = jnp.zeros((1, 128), F32)
    for at in tiles:
        sel_scores, comp_scores = ahead
        if at + ROW_TILE < rows:
            ahead = score(at + ROW_TILE)
        seen = finish(at, jnp.exp2(sel_scores * factor), jnp.exp2(comp_scores * factor), 1.0)
        range_seen = jnp.maximum(range_seen, seen)

    @pl.when(jnp.logical_not(jnp.max(range_seen) < SAFE_RANGE))
    def _():
        for at in tiles:
            sel_scores, comp_scores = score(at)
            sel_peak = jnp.max(sel_scores, axis=-1, keepdims=True)
            comp_peak = jnp.maximum(jnp.max(comp_scores, axis=-1, keepdims=True), 0.0)
            finish(
                at,
                jnp.exp2((sel_scores - sel_peak) * factor),
                jnp.exp2((comp_scores - comp_peak) * factor),
                jnp.exp2(-comp_peak * factor),
            )


def partial_logits(hidden_in, gate_weight):
    return lax.dot_general(
        gate_weight, hidden_in, (((0,), (1,)), ((), ())), preferred_element_type=F32
    )


def gate_logits(partial_value):
    parts = lax.axis_size("head")
    mine = lax.axis_index("head")
    columns = partial_value.shape[0] // parts

    def chunk(which):
        return lax.dynamic_slice_in_dim(partial_value, lax.rem(which, parts) * columns, columns, 0)

    others = [
        lax.ppermute(chunk(mine + steps), "head", [(n, (n + steps) % parts) for n in range(parts)])
        for steps in range(1, parts)
    ]
    others = lax.optimization_barrier(others)
    return chunk(mine) + others[0] + others[1] + others[2]


def send(value, perm):
    return lax.ppermute(value, "ctx", perm)


def gather_line(key_value):
    ahead = send(key_value, perm=first_axis(-1))
    behind = send(key_value, perm=first_axis(1))
    across = send(key_value, perm=first_axis(2))
    return [key_value, ahead, across, behind]


def gather_pieces(line, meanwhile, beside):
    line = jnp.concatenate(line, axis=0)
    next_line = send(line, perm=second_axis(-1))
    last_line = send(line, perm=second_axis(1))
    done = meanwhile()
    next_line, last_line, again, done = lax.optimization_barrier((next_line, last_line, line, done))
    across_line = send(again, perm=second_axis(2))
    across_line, small = lax.optimization_barrier((across_line, beside(done)))
    mine = [line, next_line, across_line, last_line]
    pieces = mine + [send(piece, perm=other_core()) for piece in mine]
    return pieces, [n * line.shape[0] for n in range(len(pieces))], small, done


def row_of_block(block, index, blocks_here, block_len):
    shard = block // blocks_here
    core = shard % CORES
    across_x = (shard // (SIDE * CORES) - index // (SIDE * CORES)) % SIDE
    across_z = (shard // CORES - index // CORES) % SIDE
    along = jnp.where(core == 0, across_z, across_x)
    line = jnp.where(core == 0, across_x, across_z)
    piece = jnp.where(core == index % CORES, 0, SIDE) + line
    return ((piece * SIDE + along) * blocks_here + block % blocks_here) * block_len


def run_near(index, queries, previous, own, heads):
    all_rows, head_dim = queries.shape
    rows_here = own.shape[0]
    whole = pl.BlockSpec((rows_here, 2 * head_dim), lambda b, *_: (0, 0))
    tile = pl.BlockSpec((NEAR_TOKENS * heads, head_dim), lambda b, *_: (b, 0))
    steps = rows_here // NEAR_TOKENS
    return pl.pallas_call(
        functools.partial(near_kernel, heads),
        out_shape=pltpu.HBM((all_rows, head_dim), F32),
        grid_spec=pltpu.PrefetchScalarGridSpec(
            num_scalar_prefetch=1,
            grid=(steps,),
            in_specs=[tile, whole, whole],
            out_specs=tile,
            scratch_shapes=[
                pltpu.VMEM((rows_here + WINDOW_TOKENS, 2 * head_dim), BF16),
                pltpu.VMEM((WINDOW_TOKENS + NEAR_TOKENS, 128), BF16),
            ],
        ),
        compiler_params=pltpu.CompilerParams(vmem_limit_bytes=24 << 20),
        cost_estimate=pl.CostEstimate(
            flops=steps * 8 * NEAR_TOKENS * heads * head_dim * 1024,
            transcendentals=0,
            bytes_accessed=steps * NEAR_TOKENS * heads * head_dim * 6,
        ),
        name="near",
    )(index, queries, previous, own)


def run_far(chosen, source_rows, index, queries, logits, win, ids_by_slot, compress_w, pieces, places):
    all_rows, head_dim = queries.shape
    blocks_here, branches, heads, block_len = logits.shape
    picks = chosen.shape[0] // blocks_here
    total_blocks = ids_by_slot.shape[1]
    tile = pl.BlockSpec((block_len * heads, head_dim), lambda b, *_: (b, 0))
    whole = lambda shape: pl.BlockSpec(shape, lambda b, *_: (0, 0))
    return pl.pallas_call(
        functools.partial(far_kernel, block_len, heads, picks, places),
        out_shape=jax.ShapeDtypeStruct((all_rows, head_dim), BF16),
        grid_spec=pltpu.PrefetchScalarGridSpec(
            num_scalar_prefetch=3,
            grid=(blocks_here,),
            in_specs=[
                tile,
                pl.BlockSpec((1, branches, heads, block_len), lambda b, *_: (b, 0, 0, 0)),
                tile,
                whole((1, total_blocks)),
                whole((block_len, 2 * head_dim)),
            ]
            + [pl.BlockSpec(memory_space=pl.ANY)] * len(pieces),
            out_specs=tile,
            scratch_shapes=[
                pltpu.VMEM((total_blocks * block_len, 2 * head_dim), BF16),
                pltpu.VMEM((2, total_blocks, 2 * head_dim), BF16),
                pltpu.VMEM((picks * block_len, 2 * head_dim), BF16),
                pltpu.VMEM((picks * block_len, 2 * head_dim), BF16),
                pltpu.SemaphoreType.DMA((len(pieces),)),
            ],
        ),
        compiler_params=pltpu.CompilerParams(vmem_limit_bytes=28 << 20),
        cost_estimate=pl.CostEstimate(
            flops=8 * all_rows * head_dim * 1280, transcendentals=all_rows * 1280, bytes_accessed=20 << 20
        ),
        name="far",
    )(
        chosen, source_rows, index, queries, logits, in_hbm(win), ids_by_slot, compress_w,
        *pieces,
    )


def body(
    hidden_in,
    gate_weight,
    encoded_queries,
    encoded_keys,
    value_tensor,
    comp_key_weight,
    comp_value_weight,
    selection,
):
    rows_here, heads_here, head_dim = encoded_queries.shape
    block_len = comp_key_weight.shape[0]
    blocks_here = rows_here // block_len
    shard_parts = lax.axis_size("ctx")
    all_rows = rows_here * heads_here
    place_here = lax.axis_index("ctx").astype(jnp.int32)
    index = place_here.reshape(1)

    key_value = jnp.concatenate([encoded_keys, value_tensor], axis=-1).reshape(rows_here, 2 * head_dim)
    line = gather_line(key_value)
    previous = send(key_value, perm=[(n, n + 1) for n in range(shard_parts - 1)])
    compress_w = jnp.concatenate([comp_key_weight, comp_value_weight], axis=-1)
    queries = in_hbm(encoded_queries.reshape(all_rows, head_dim))
    total_blocks = blocks_here * shard_parts
    chosen = selection.reshape(-1)
    source_rows = row_of_block(chosen, place_here, blocks_here, block_len)
    block_ids = jnp.arange(total_blocks, dtype=jnp.int32)
    placed = row_of_block(block_ids, place_here, blocks_here, block_len) // block_len
    slots = jnp.arange(total_blocks, dtype=jnp.int32)
    ids_by_slot = jnp.sum(
        jnp.where(placed[None, :] == slots[:, None], block_ids[None, :], 0), axis=1, dtype=jnp.int32
    ).reshape(1, total_blocks)

    early, chosen, source_rows, ids_by_slot, compress_w = lax.optimization_barrier(
        (index, chosen, source_rows, ids_by_slot, compress_w)
    )
    near = functools.partial(run_near, early, queries, previous, key_value, heads_here)

    def late_inputs(win):
        after, _ = lax.optimization_barrier((hidden_in, win))
        logits = gate_logits(partial_logits(after, gate_weight))
        logits = logits.reshape(heads_here, 3, blocks_here, block_len).transpose(2, 1, 0, 3)
        return chosen, source_rows, logits, ids_by_slot, compress_w

    pieces, places, (picked, picked_rows, logits, slot_ids, weights), win = gather_pieces(line, near, late_inputs)
    out = run_far(picked, picked_rows, index, queries, logits, win, slot_ids, weights, pieces, places)
    return out.reshape(rows_here, heads_here, head_dim)


def solution(mesh):
    return jax.shard_map(
        body,
        mesh=mesh,
        in_specs=(
            P("ctx", "head"),
            P("head", None),
            P("ctx", "head", None),
            P("ctx", "head", None),
            P("ctx", "head", None),
            P(),
            P(),
            P("ctx", "head", None),
        ),
        out_specs=P("ctx", "head", None),
        check_vma=False,
    )
```
